256 devices in a mesh: ctx: 16 (over y, x), head: 4 (over z_hi, core), dp: 4 (over z_lo).
Axes of the slice: x: 4, y: 4, z: 8 (z_hi: 2, z_lo: 4; z = z_hi * 4 + z_lo), core: 2. Of those that a mesh axis runs over, the one named last changes fastest.
Arguments:
- queries: bfloat16 [4096, 8, 8, 128], P('ctx', 'head', 'dp'), may hold values from -2.5 to 2.5
- key_rows: bfloat16 [4096, 8, 128], P(('ctx', 'dp'), 'head'), may hold values from -2.5 to 2.5
- value_rows: bfloat16 [4096, 8, 128], P(('ctx', 'dp'), 'head'), may hold values from -6 to 6
- forward_out: bfloat16 [4096, 8, 8, 128], P('ctx', 'head', 'dp'), may hold values from -0.59765625 to 0.59765625
- grad_out: bfloat16 [4096, 8, 8, 128], P('ctx', 'head', 'dp'), may hold values from -24 to 24
- logsumexp: float32 [8, 8, 4096], P('head', 'dp', 'ctx'), as said below
- selected: int32 [16, 8, 8, 8], P('ctx', 'head', 'dp'), may hold values from -1 to 15, as said below
Outputs:
- query_grad: bfloat16 [4096, 8, 8, 128], P('ctx', 'head', 'dp')
- key_grad: float32 [4096, 8, 128], P(('ctx', 'dp'), 'head')
- value_grad: float32 [4096, 8, 128], P(('ctx', 'dp'), 'head')
The draws below stay inside these ranges and needn't reach their ends.
Inputs may be any that keep to these rules, and one draw needn't show every extreme that they name: selected[i, a, g, 0] = i. The other entries of a row are distinct blocks below i (some blocks below i may be left out), followed by -1 in the slots that remain. `logsumexp`: each entry lies between log(512) and log(512) + 1.5.
All inputs are finite; a program needn't handle non-finite values.
Results may differ from the reference program's by a relative error of at most 0.0051.
Values may be sent and summed in bfloat16 or wider, within the bound.
No kernel may reach another device: no remote copies, remote signals or barrier semaphores. Data moves between devices by JAX's collectives and lax.ppermute only.
A program may use at most 64 MiB of HBM per device.

```python
import math
import jax
import jax.numpy as jnp
from jax import lax

HEAD_DIM = 128
KV_HEADS = 8
BLOCK = 256
TOPK = 8
GROUP = 8
BLOCKS = 16
TOKENS = 4096


def draw_logsumexp(key, part):
    base_level = math.log(2.0 * BLOCK)
    scattered_piece = jax.random.uniform(key, (KV_HEADS, GROUP, TOKENS), jnp.float32, 0.0, 1.5)
    return (base_level + scattered_piece).astype(jnp.float32)


def draw_selected(key, part):
    option_count = max(BLOCKS, TOPK)
    block_options = jnp.arange(option_count, dtype=jnp.int32)
    own_block = jnp.arange(BLOCKS, dtype=jnp.int32)[:, None, None, None]
    jitter_values = jax.random.randint(key, (BLOCKS, KV_HEADS, GROUP, option_count), 0, 1 << 20, dtype=jnp.int32)
    preference = jax.random.randint(jax.random.fold_in(key, 11), (BLOCKS, KV_HEADS, GROUP, 1), 0, 2, dtype=jnp.int32)
    eligible = jax.random.randint(jax.random.fold_in(key, 23), (BLOCKS, KV_HEADS, GROUP, option_count), 0, 4, dtype=jnp.int32) != 0
    extra_score = preference * (block_options == 0).astype(jnp.int32) * (option_count << 20)
    score_rows = jitter_values * option_count + block_options + extra_score
    score_rows = jnp.where((block_options < own_block) & eligible, score_rows, -1 - block_options)
    values, chosen = lax.top_k(score_rows, TOPK - 1)
    chosen = jnp.where(values >= 0, chosen, -1).astype(jnp.int32)
    own_slot = jnp.broadcast_to(own_block, (BLOCKS, KV_HEADS, GROUP, 1)).astype(jnp.int32)
    return jnp.concatenate([own_slot, chosen], axis=-1)


def block_scale(key, shape, split, low, high):
    loudness = 1.0
    for dim, blocks in split:
        draws = jax.random.uniform(jax.random.fold_in(jax.random.fold_in(key, 6), dim), (blocks,), jnp.float32, low / len(split), high / len(split))
        loudness = loudness * jnp.repeat(jnp.exp(draws), shape[dim] // blocks).reshape((-1,) + (1,) * (len(shape) - 1 - dim))
    return loudness


def scatter_about(stream_key, dims, width, limit, split=(), kind=jnp.bfloat16):
    loudness = block_scale(stream_key, dims, split, -0.22, 0.18) if split else 1.0
    array = jax.random.normal(stream_key, dims, jnp.float32) * width * loudness
    return jnp.minimum(jnp.maximum(array, -limit), limit).astype(kind)


def setup_inputs(seed: int = 0) -> dict:
    keys = jax.random.split(jax.random.key(seed), 8)
    queries = scatter_about(keys[0], (TOKENS, KV_HEADS, GROUP, HEAD_DIM), 1.0, 2.5, ((0, 16), (1, 4), (2, 4)))
    key_rows = scatter_about(keys[1], (TOKENS, KV_HEADS, HEAD_DIM), 1.0, 2.5, ((0, 64), (1, 4)))
    value_rows = scatter_about(keys[2], (TOKENS, KV_HEADS, HEAD_DIM), 1.0, 6.0, ((0, 64), (1, 4)))
    forward_out = scatter_about(keys[3], (TOKENS, KV_HEADS, GROUP, HEAD_DIM), 0.1, 0.59765625, ((0, 16), (1, 4), (2, 4)))
    grad_out = scatter_about(keys[4], (TOKENS, KV_HEADS, GROUP, HEAD_DIM), 4.0, 24.0, ((0, 16), (1, 4), (2, 4)))
    logsumexp = draw_logsumexp(jax.random.fold_in(keys[7], 71), 0)
    selected = draw_selected(jax.random.fold_in(keys[7], 71), 0)
    return {"queries": queries, "key_rows": key_rows, "value_rows": value_rows, "forward_out": forward_out, "grad_out": grad_out, "logsumexp": logsumexp, "selected": selected}


def block_terms(query_blk, grad_blk, lse_row, delta_part, slot_ids, key_view, value_layout, head_local, slot_offset, softmax_scale):
    slot_count = slot_ids.shape[0]
    block_len = query_blk.shape[0]
    safe_ids = jnp.maximum(slot_ids, 0)
    positions = jnp.arange(block_len, dtype=jnp.int32)
    key_sel = key_view[safe_ids[:, None], positions[None, :], head_local].reshape(slot_count * block_len, -1)
    value_sel = value_layout[safe_ids[:, None], positions[None, :], head_local].reshape(slot_count * block_len, -1)
    columns = jnp.arange(slot_count * block_len, dtype=jnp.int32)
    slot_of = columns // block_len
    within = columns % block_len
    filled = slot_ids[slot_of] >= 0
    causal = (slot_of + slot_offset != 0)[None, :] | (within[None, :] <= positions[:, None])
    keep = filled[None, :] & causal
    score_rows = lax.dot_general(query_blk, key_sel, (((1,), (1,)), ((), ())), preferred_element_type=jnp.float32) * softmax_scale
    probs = jnp.where(keep, jnp.exp(score_rows - lse_row[:, None]), jnp.float32(0.0))
    probs_low = probs.astype(jnp.bfloat16)
    value_part = lax.dot_general(probs_low, grad_blk, (((0,), (0,)), ((), ())), preferred_element_type=jnp.float32)
    dprobs = lax.dot_general(grad_blk, value_sel, (((1,), (1,)), ((), ())), preferred_element_type=jnp.float32)
    dscores = (probs * (dprobs - delta_part[:, None]) * softmax_scale).astype(jnp.bfloat16)
    query_part = jnp.dot(dscores, key_sel, preferred_element_type=jnp.float32)
    key_part = lax.dot_general(dscores, query_blk, (((0,), (0,)), ((), ())), preferred_element_type=jnp.float32)
    return query_part, key_part.reshape(slot_count, block_len, -1), value_part.reshape(slot_count, block_len, -1)


def reference(queries, key_rows, value_rows, forward_out, grad_out, logsumexp, selected):
    softmax_scale = HEAD_DIM ** -0.5
    delta_rows = jnp.sum(grad_out.astype(jnp.float32) * forward_out.astype(jnp.float32), axis=-1)
    key_view = key_rows.reshape(BLOCKS, BLOCK, KV_HEADS, HEAD_DIM)
    value_layout = value_rows.reshape(BLOCKS, BLOCK, KV_HEADS, HEAD_DIM)
    positions = jnp.arange(BLOCK, dtype=jnp.int32)

    def head_step(carried, item_index):
        key_acc, value_acc = carried
        block_index = (item_index // (KV_HEADS * GROUP)).astype(jnp.int32)
        head_local = ((item_index // GROUP) % KV_HEADS).astype(jnp.int32)
        group_index = (item_index % GROUP).astype(jnp.int32)
        zero_index = jnp.zeros((), jnp.int32)
        row_start = (block_index * BLOCK).astype(jnp.int32)
        query_blk = lax.dynamic_slice(queries, (row_start, head_local, group_index, zero_index), (BLOCK, 1, 1, HEAD_DIM)).reshape(BLOCK, HEAD_DIM)
        grad_blk = lax.dynamic_slice(grad_out, (row_start, head_local, group_index, zero_index), (BLOCK, 1, 1, HEAD_DIM)).reshape(BLOCK, HEAD_DIM)
        lse_row = lax.dynamic_slice(logsumexp, (head_local, group_index, row_start), (1, 1, BLOCK)).reshape(BLOCK)
        delta_part = lax.dynamic_slice(delta_rows, (row_start, head_local, group_index), (BLOCK, 1, 1)).reshape(BLOCK)
        slot_ids = lax.dynamic_slice(selected, (block_index, head_local, group_index, zero_index), (1, 1, 1, TOPK)).reshape(TOPK)
        query_part, key_part, value_part = block_terms(query_blk, grad_blk, lse_row, delta_part, slot_ids, key_view, value_layout, head_local, 0, softmax_scale)
        target_ids = jnp.where(slot_ids >= 0, slot_ids, BLOCKS).astype(jnp.int32)
        key_acc = key_acc.at[target_ids[:, None], positions[None, :], head_local].add(key_part, mode="drop")
        value_acc = value_acc.at[target_ids[:, None], positions[None, :], head_local].add(value_part, mode="drop")
        return (key_acc, value_acc), query_part.astype(jnp.bfloat16)

    empty = jnp.zeros((BLOCKS, BLOCK, KV_HEADS, HEAD_DIM), jnp.float32)
    items = jnp.arange(BLOCKS * KV_HEADS * GROUP, dtype=jnp.int32)
    (key_acc, value_acc), query_blocks = lax.scan(head_step, (empty, empty), items)
    query_grad = query_blocks.reshape(BLOCKS, KV_HEADS, GROUP, BLOCK, HEAD_DIM).transpose(0, 3, 1, 2, 4).reshape(TOKENS, KV_HEADS, GROUP, HEAD_DIM)
    key_grad = key_acc.reshape(TOKENS, KV_HEADS, HEAD_DIM)
    value_grad = value_acc.reshape(TOKENS, KV_HEADS, HEAD_DIM)
    return (query_grad, key_grad, value_grad)
```

```python
import jax
import jax.numpy as jnp
from jax import lax
from jax.experimental import pallas as pl
from jax.experimental.pallas import tpu as pltpu
from jax.sharding import PartitionSpec as P

BLOCK = 256
SIDE = 4


def shifts(rows, columns):
    return [
        (y * SIDE + x, (y + rows) % SIDE * SIDE + (x + columns) % SIDE)
        for y in range(SIDE)
        for x in range(SIDE)
    ]


def move(array, rows, columns):
    return lax.ppermute(array, "ctx", shifts(rows, columns))


def swap(array, bit):
    return lax.ppermute(array, "dp", [(d, d ^ bit) for d in range(4)])


def gather_axis(own, rows, columns):
    before = move(own, rows, columns)
    after = move(own, -rows, -columns)
    far = move(before, rows, columns)
    return [own, before, far, after]


def reduce_axis(terms, rows, columns):
    far = move(terms[2], -rows, -columns)
    after = move(terms[3], rows, columns)
    near = (terms[1].astype(jnp.float32) + far.astype(jnp.float32)).astype(jnp.bfloat16)
    before = move(near, -rows, -columns)
    return (
        terms[0].astype(jnp.float32)
        + after.astype(jnp.float32)
        + before.astype(jnp.float32)
    )


def attend(
    sel, place, stats, qd_own, qd_far, *refs, scale, blocks
):
    k_in, v_in = refs[0:SIDE], refs[SIDE : 2 * SIDE]
    k_out, v_out = refs[2 * SIDE : 3 * SIDE], refs[3 * SIDE : 4 * SIDE]
    dq_own, dq_far = refs[4 * SIDE : 4 * SIDE + 2]
    (keys, vals, q_t, do_t, k_t, dk_low, dv_low, acc_k, acc_v, dq_t, count, members, sems) = refs[
        4 * SIDE + 2 :
    ]
    copies = []
    for d in range(SIDE):
        span = pl.ds(d * SIDE, SIDE)
        copies.append(pltpu.make_async_copy(k_in[d], keys.at[span], sems.at[d]))
        copies.append(pltpu.make_async_copy(v_in[d], vals.at[span], sems.at[SIDE + d]))
    for copy in copies:
        copy.start()

    row, column = place[0], place[1]
    for r in range(blocks):
        count[r] = 0
    for g in range(4):
        for s in range(1, sel.shape[1]):
            block = sel[g, s]

            @pl.when(block >= 0)
            def _(block=block, g=g):
                rel = ((row - (block >> 2)) & 3) * SIDE + ((column - (block & 3)) & 3)
                at = count[rel]
                members[rel * 4 + at] = g
                count[rel] = at + 1

    for half, qd in enumerate((qd_own, qd_far)):
        for g in range(2):
            q_t[2 * half + g] = qd[0, g].T
            do_t[2 * half + g] = qd[1, g].T
    dq_t[...] = jnp.zeros_like(dq_t)
    for copy in copies:
        copy.wait()

    def item(k, v, q, do, g, causal):
        lse = stats[pl.ds(g, 1), :]
        delta = stats[pl.ds(g + 4, 1), :]
        scores = jnp.dot(k, q_t[g], preferred_element_type=jnp.float32) * scale
        probs = jnp.exp(scores - lse)
        if causal:
            at_key = lax.broadcasted_iota(jnp.int32, probs.shape, 0)
            at_query = lax.broadcasted_iota(jnp.int32, probs.shape, 1)
            probs = jnp.where(at_key <= at_query, probs, 0.0)
        low = probs.astype(jnp.bfloat16)
        dprobs = jnp.dot(v, do_t[g], preferred_element_type=jnp.float32)
        dscores = (probs * (dprobs - delta) * scale).astype(jnp.bfloat16)
        acc_v[...] += jnp.dot(low, do, preferred_element_type=jnp.float32)
        acc_k[...] += jnp.dot(dscores, q, preferred_element_type=jnp.float32)
        dq_t[g] += jnp.dot(k_t[...], dscores, preferred_element_type=jnp.float32)

    def visit(r, g, causal):
        rv = (r % SIDE) * SIDE + r // SIDE
        k, v = keys[r], vals[rv]

        @pl.when(g < 2)
        def _():
            item(k, v, qd_own[0, g], qd_own[1, g], g, causal)

        @pl.when(g >= 2)
        def _():
            item(k, v, qd_far[0, g - 2], qd_far[1, g - 2], g, causal)

    def clear(r):
        acc_k[...] = jnp.zeros_like(acc_k)
        acc_v[...] = jnp.zeros_like(acc_v)
        k_t[...] = keys[r].T

    def flush(r):
        rv = (r % SIDE) * SIDE + r // SIDE
        dk_low[r] = acc_k[...].astype(jnp.bfloat16)
        dv_low[rv] = acc_v[...].astype(jnp.bfloat16)

    clear(0)

    @pl.loop(0, 4)
    def _(g):
        visit(0, g, True)

    flush(0)

    @pl.loop(1, blocks)
    def _(r):
        clear(r)

        @pl.loop(0, count[r])
        def _(n):
            visit(r, members[r * 4 + n], False)

        flush(r)

    for g in range(2):
        dq_own[g] = dq_t[g].T.astype(jnp.bfloat16)
        dq_far[g] = dq_t[2 + g].T.astype(jnp.bfloat16)
    copies = []
    for d in range(SIDE):
        span = pl.ds(d * SIDE, SIDE)
        copies.append(pltpu.make_async_copy(dk_low.at[span], k_out[d], sems.at[d]))
        copies.append(pltpu.make_async_copy(dv_low.at[span], v_out[d], sems.at[SIDE + d]))
    for copy in copies:
        copy.start()
    for copy in copies:
        copy.wait()


def attend_call(sel, place, stats, qd_own, qd_far, key_parts, value_parts, head_dim):
    blocks = SIDE * SIDE
    vmem = pl.BlockSpec(memory_space=pltpu.VMEM)
    smem = pl.BlockSpec(memory_space=pltpu.SMEM)
    anywhere = pl.BlockSpec(memory_space=pl.ANY)
    low, full = jnp.bfloat16, jnp.float32
    part = jax.ShapeDtypeStruct((SIDE, BLOCK, head_dim), low)
    dq = jax.ShapeDtypeStruct((2, BLOCK, head_dim), low)
    outs = pl.pallas_call(
        lambda *refs: attend(*refs, scale=head_dim**-0.5, blocks=blocks),
        out_shape=[part] * 8 + [dq] * 2,
        in_specs=[smem, smem, vmem, vmem, vmem] + [anywhere] * 8,
        out_specs=[anywhere] * 8 + [vmem] * 2,
        scratch_shapes=[
            pltpu.VMEM((blocks, BLOCK, head_dim), low),
            pltpu.VMEM((blocks, BLOCK, head_dim), low),
            pltpu.VMEM((4, head_dim, BLOCK), low),
            pltpu.VMEM((4, head_dim, BLOCK), low),
            pltpu.VMEM((head_dim, BLOCK), low),
            pltpu.VMEM((blocks, BLOCK, head_dim), low),
            pltpu.VMEM((blocks, BLOCK, head_dim), low),
            pltpu.VMEM((BLOCK, head_dim), full),
            pltpu.VMEM((BLOCK, head_dim), full),
            pltpu.VMEM((4, head_dim, BLOCK), full),
            pltpu.SMEM((blocks,), jnp.int32),
            pltpu.SMEM((4 * blocks,), jnp.int32),
            pltpu.SemaphoreType.DMA((8,)),
        ],
        name="attend",
        cost_estimate=pl.CostEstimate(
            flops=32 * 5 * 2 * BLOCK * BLOCK * head_dim,
            bytes_accessed=10 << 20,
            transcendentals=32 * BLOCK * BLOCK,
        ),
    )(sel, place, stats, qd_own, qd_far, *key_parts, *value_parts)
    return outs[0:4], outs[4:8], outs[8], outs[9]


def local(queries, key_rows, value_rows, forward_out, grad_out, logsumexp, selected):
    head_dim = queries.shape[-1]
    low, full = jnp.bfloat16, jnp.float32
    ctx, dp = lax.axis_index("ctx"), lax.axis_index("dp")
    parity, upper = dp % 2, dp // 2
    even, lower = parity == 0, upper == 0

    def mine(pair):
        return jnp.where(even, pair[0], pair[1])

    def other(pair):
        return jnp.where(even, pair[1], pair[0])

    kv = jnp.stack([key_rows, value_rows]).transpose(2, 0, 1, 3)
    near = swap(other(kv), 1)
    own = mine(kv)
    pair = jnp.where(even, jnp.concatenate([own, near], 1), jnp.concatenate([near, own], 1))
    far = swap(pair, 2)
    kv = jnp.where(lower, jnp.concatenate([pair, far], 1), jnp.concatenate([far, pair], 1))

    keys = jnp.stack(gather_axis(kv[0], 0, 1))
    values = jnp.stack(gather_axis(kv[1], 1, 0))
    key_parts = gather_axis(keys, 1, 0)
    value_parts = gather_axis(values, 0, 1)

    qd = jnp.stack([queries, grad_out]).transpose(2, 0, 3, 1, 4)
    qd_far = swap(other(qd), 1)
    qd_own = mine(qd)
    delta = jnp.sum(grad_out.astype(full) * forward_out.astype(full), axis=-1).transpose(1, 2, 0)
    ids = jnp.pad(selected[0].astype(full), ((0, 0), (0, 0), (0, BLOCK - selected.shape[-1])))
    small = jnp.stack([logsumexp, delta, ids], axis=1)
    small_far = swap(other(small), 1)
    small = jnp.concatenate([mine(small), small_far], axis=1)
    stats = small[0:2].reshape(8, BLOCK)
    sel = small[2, :, : selected.shape[-1]].astype(jnp.int32)
    place = jnp.stack([ctx // SIDE, ctx % SIDE]).astype(jnp.int32)

    dk, dv, dq_own, dq_far = attend_call(
        sel, place, stats, qd_own, qd_far, key_parts, value_parts, head_dim
    )

    dq_far = swap(dq_far, 1)
    query_grad = jnp.where(
        even, jnp.stack([dq_own, dq_far]), jnp.stack([dq_far, dq_own])
    ).transpose(2, 0, 1, 3)

    dk = reduce_axis(dk, 1, 0).astype(low)
    dv = reduce_axis(dv, 0, 1).astype(low)
    dk = reduce_axis([dk[d] for d in range(SIDE)], 0, 1)
    dv = reduce_axis([dv[d] for d in range(SIDE)], 1, 0)

    grads = jnp.stack([dk, dv]).reshape(2, 2, 2, BLOCK // 4, head_dim)
    keep = jnp.where(lower, grads[:, 0], grads[:, 1])
    send = jnp.where(lower, grads[:, 1], grads[:, 0]).astype(low)
    keep = keep + swap(send, 2).astype(full)
    own = jnp.where(even, keep[:, 0], keep[:, 1])
    near = swap(jnp.where(even, keep[:, 1], keep[:, 0]), 1)
    both = jnp.where(even, jnp.stack([own, near], 2), jnp.stack([near, own], 2))
    return (query_grad, both[0], both[1])


def solution(mesh):
    return jax.shard_map(
        local,
        mesh=mesh,
        in_specs=(
            P("ctx", "head", "dp", None),
            P(("ctx", "dp"), "head", None),
            P(("ctx", "dp"), "head", None),
            P("ctx", "head", "dp", None),
            P("ctx", "head", "dp", None),
            P("head", "dp", "ctx"),
            P("ctx", "head", "dp", None),
        ),
        out_specs=(
            P("ctx", "head", "dp", None),
            P(("ctx", "dp"), "head", None),
            P(("ctx", "dp"), "head", None),
        ),
        check_vma=False,
    )
```

```python
import jax
import jax.numpy as jnp
from jax import lax
from jax.experimental import pallas as pl
from jax.experimental.pallas import tpu as pltpu
from jax.sharding import PartitionSpec as P

BLOCK = 256
SIDE = 4


def shifts(rows, columns):
    return [
        (y * SIDE + x, (y + rows) % SIDE * SIDE + (x + columns) % SIDE)
        for y in range(SIDE)
        for x in range(SIDE)
    ]


def move(array, rows, columns):
    return lax.ppermute(array, "ctx", shifts(rows, columns))


def swap(array, bit):
    return lax.ppermute(array, "dp", [(d, d ^ bit) for d in range(4)])


def gather_small(own, rows, columns):
    before = move(own, rows, columns)
    after = move(own, -rows, -columns)
    far = move(own, 2 * rows, 2 * columns)
    return [own, before, far, after]


def gather_large(own, rows, columns):
    half = own.shape[0] // 2
    before = move(own, rows, columns)
    after = move(own, -rows, -columns)
    far_low = move(before[:half], rows, columns)
    far_high = move(after[half:], -rows, -columns)
    return [own, before, after, far_low, far_high]


def reduce_large(own, before, after, far_low, far_high, rows, columns):
    full, half = jnp.float32, far_low.shape[0]
    low_far = move(far_low, -rows, -columns)
    high_far = move(far_high, rows, columns)
    first = (before[:half].astype(full) + low_far.astype(full)).astype(before.dtype)
    second = (after[half:].astype(full) + high_far.astype(full)).astype(after.dtype)
    before = move(jnp.concatenate([first, before[half:]]), -rows, -columns)
    after = move(jnp.concatenate([after[:half], second]), rows, columns)
    return own.astype(full) + before.astype(full) + after.astype(full)


def reduce_small(terms, rows, columns):
    full = jnp.float32
    low = terms.astype(jnp.bfloat16)
    far = move(low[2], -2 * rows, -2 * columns)
    before = move(low[1], -rows, -columns)
    after = move(low[3], rows, columns)
    return terms[0] + far.astype(full) + before.astype(full) + after.astype(full)


PARTS = ((0, SIDE), (SIDE, SIDE), (3 * SIDE, SIDE), (2 * SIDE, SIDE // 2), (2 * SIDE + SIDE // 2, SIDE // 2))


def attend(sel, place, stats, qd_own, qd_far, *refs, scale, blocks):
    count = len(PARTS)
    k_in, v_in = refs[0:count], refs[count : 2 * count]
    k_out, v_out = refs[2 * count : 3 * count], refs[3 * count : 4 * count]
    dq_own, dq_far = refs[4 * count : 4 * count + 2]
    (
        keys,
        vals,
        keys_t,
        q,
        do,
        q_t,
        do_t,
        p_even,
        s_even,
        p_odd,
        s_odd,
        acc_k,
        acc_v,
        dk_low,
        dv_low,
        dq_t,
        item_block,
        item_member,
        sems,
    ) = refs[4 * count + 2 :]
    copies = []
    for n, (first, size) in enumerate(PARTS):
        span = pl.ds(first, size)
        copies.append(pltpu.make_async_copy(k_in[n], keys.at[span], sems.at[n]))
        copies.append(pltpu.make_async_copy(v_in[n], vals.at[span], sems.at[count + n]))
    for copy in copies:
        copy.start()

    row, column = place[0], place[1]
    for g in range(4):
        item_block[g] = 0
        item_member[g] = g
    total = jnp.int32(4)
    for g in range(4):
        for s in range(1, sel.shape[1]):
            block = sel[g, s]
            rel = ((row - (block >> 2)) & 3) * SIDE + ((column - (block & 3)) & 3)
            item_block[total] = rel
            item_member[total] = g
            total = total + (block >= 0).astype(jnp.int32)
    item_block[total] = 0
    item_member[total] = 4

    for half, qd in enumerate((qd_own, qd_far)):
        for g in range(2):
            q[2 * half + g] = qd[0, g]
            do[2 * half + g] = qd[1, g]
            q_t[2 * half + g] = qd[0, g].T
            do_t[2 * half + g] = qd[1, g].T
    dq_t[...] = jnp.zeros_like(dq_t)

    @pl.loop(0, blocks)
    def _(r):
        acc_k[r] = jnp.zeros(acc_k.shape[1:], jnp.float32)
        acc_v[r] = jnp.zeros(acc_v.shape[1:], jnp.float32)

    for copy in copies:
        copy.wait()

    @pl.loop(0, blocks)
    def _(r):
        keys_t[r] = keys[r].T

    offset = lax.broadcasted_iota(jnp.int32, (BLOCK, BLOCK), 0) - lax.broadcasted_iota(
        jnp.int32, (BLOCK, BLOCK), 1
    )

    def weigh(n, p_buf, s_buf):
        r, m = item_block[n], item_member[n]
        g = m & 3
        rv = (r & 3) * SIDE + (r >> 2)
        lse = stats[pl.ds(m, 1), :]
        delta = stats[pl.ds(g + 8, 1), :]
        allowed = jnp.where(r == 0, 0, BLOCK)
        scores = jnp.dot(keys[r], q_t[g], preferred_element_type=jnp.float32) * scale
        probs = jnp.where(offset <= allowed, jnp.exp(scores - lse), 0.0)
        p_buf[...] = probs.astype(jnp.bfloat16)
        dprobs = jnp.dot(vals[rv], do_t[g], preferred_element_type=jnp.float32)
        s_buf[...] = (probs * (dprobs - delta) * scale).astype(jnp.bfloat16)

    def spread(n, p_buf, s_buf):
        r, g = item_block[n], item_member[n] & 3
        rv = (r & 3) * SIDE + (r >> 2)
        acc_v[rv] += jnp.dot(p_buf[...], do[g], preferred_element_type=jnp.float32)
        acc_k[r] += jnp.dot(s_buf[...], q[g], preferred_element_type=jnp.float32)
        dq_t[g] += jnp.dot(keys_t[r], s_buf[...], preferred_element_type=jnp.float32)

    weigh(0, p_even, s_even)
    pairs = (total + 1) >> 1

    @pl.loop(0, pairs - 1)
    def _(i):
        weigh(2 * i + 1, p_odd, s_odd)
        spread(2 * i, p_even, s_even)
        weigh(2 * i + 2, p_even, s_even)
        spread(2 * i + 1, p_odd, s_odd)

    last = 2 * pairs - 2
    weigh(last + 1, p_odd, s_odd)
    spread(last, p_even, s_even)
    spread(last + 1, p_odd, s_odd)

    @pl.loop(0, blocks)
    def _(r):
        dk_low[r] = acc_k[r].astype(jnp.bfloat16)
        dv_low[r] = acc_v[r].astype(jnp.bfloat16)

    copies = []
    for n, (first, size) in enumerate(PARTS):
        span = pl.ds(first, size)
        copies.append(pltpu.make_async_copy(dk_low.at[span], k_out[n], sems.at[n]))
        copies.append(pltpu.make_async_copy(dv_low.at[span], v_out[n], sems.at[count + n]))
    for copy in copies:
        copy.start()
    for g in range(2):
        dq_own[g] = dq_t[g].T.astype(jnp.bfloat16)
        dq_far[g] = dq_t[2 + g].T.astype(jnp.bfloat16)
    for copy in copies:
        copy.wait()


def attend_call(sel, place, stats, qd_own, qd_far, key_parts, value_parts, head_dim):
    blocks = SIDE * SIDE
    vmem = pl.BlockSpec(memory_space=pltpu.VMEM)
    smem = pl.BlockSpec(memory_space=pltpu.SMEM)
    anywhere = pl.BlockSpec(memory_space=pl.ANY)
    low, full = jnp.bfloat16, jnp.float32
    parts = [jax.ShapeDtypeStruct((size, BLOCK, head_dim), low) for _, size in PARTS]
    dq = jax.ShapeDtypeStruct((2, BLOCK, head_dim), low)
    count = len(PARTS)
    outs = pl.pallas_call(
        lambda *refs: attend(*refs, scale=head_dim**-0.5, blocks=blocks),
        out_shape=parts * 2 + [dq] * 2,
        in_specs=[smem, smem, vmem, vmem, vmem] + [anywhere] * (2 * count),
        out_specs=[anywhere] * (2 * count) + [vmem] * 2,
        scratch_shapes=[
            pltpu.VMEM((blocks, BLOCK, head_dim), low),
            pltpu.VMEM((blocks, BLOCK, head_dim), low),
            pltpu.VMEM((blocks, head_dim, BLOCK), low),
            pltpu.VMEM((4, BLOCK, head_dim), low),
            pltpu.VMEM((4, BLOCK, head_dim), low),
            pltpu.VMEM((4, head_dim, BLOCK), low),
            pltpu.VMEM((4, head_dim, BLOCK), low),
            pltpu.VMEM((BLOCK, BLOCK), low),
            pltpu.VMEM((BLOCK, BLOCK), low),
            pltpu.VMEM((BLOCK, BLOCK), low),
            pltpu.VMEM((BLOCK, BLOCK), low),
            pltpu.VMEM((blocks, BLOCK, head_dim), full),
            pltpu.VMEM((blocks, BLOCK, head_dim), full),
            pltpu.VMEM((blocks, BLOCK, head_dim), low),
            pltpu.VMEM((blocks, BLOCK, head_dim), low),
            pltpu.VMEM((4, head_dim, BLOCK), full),
            pltpu.SMEM((40,), jnp.int32),
            pltpu.SMEM((40,), jnp.int32),
            pltpu.SemaphoreType.DMA((2 * count,)),
        ],
        name="attend",
        compiler_params=pltpu.CompilerParams(vmem_limit_bytes=22 << 20),
        cost_estimate=pl.CostEstimate(
            flops=32 * 5 * 2 * BLOCK * BLOCK * head_dim,
            bytes_accessed=10 << 20,
            transcendentals=32 * BLOCK * BLOCK,
        ),
    )(sel, place, stats, qd_own, qd_far, *key_parts, *value_parts)
    return outs[0:count], outs[count : 2 * count], outs[2 * count], outs[2 * count + 1]


def local(queries, key_rows, value_rows, forward_out, grad_out, logsumexp, selected):
    head_dim = queries.shape[-1]
    low, full = jnp.bfloat16, jnp.float32
    ctx, dp = lax.axis_index("ctx"), lax.axis_index("dp")
    even, lower = dp % 2 == 0, dp < 2

    def mine(pair):
        return jnp.where(even, pair[0], pair[1])

    def other(pair):
        return jnp.where(even, pair[1], pair[0])

    def ordered(parts, axis):
        a, b, c, d = parts
        join = jnp.concatenate
        near = jnp.where(even, join([a, b], axis), join([b, a], axis))
        far = jnp.where(even, join([c, d], axis), join([d, c], axis))
        return jnp.where(lower, join([near, far], axis), join([far, near], axis))

    kv = jnp.stack([key_rows, value_rows]).transpose(2, 0, 1, 3)
    own, spare = mine(kv), other(kv)
    kv = ordered([own, swap(spare, 1), swap(own, 2), swap(spare, 3)], 1)

    keys = jnp.stack(gather_small(kv[0], 0, 1))
    values = jnp.stack(gather_small(kv[1], 1, 0))
    key_parts = gather_large(keys, 1, 0)
    value_parts = gather_large(values, 0, 1)

    qd = jnp.stack([queries, grad_out]).transpose(2, 0, 3, 1, 4)
    qd_far = swap(other(qd), 1)
    qd_own = mine(qd)
    delta = jnp.sum(grad_out.astype(full) * forward_out.astype(full), axis=-1).transpose(1, 2, 0)
    ids = jnp.pad(selected[0].astype(full), ((0, 0), (0, 0), (0, BLOCK - selected.shape[-1])))
    small = jnp.stack([logsumexp, delta, ids], axis=1)
    small_far = swap(other(small), 1)
    small = jnp.concatenate([mine(small), small_far], axis=1)
    never = jnp.full((4, BLOCK), 1e30, full)
    stats = jnp.concatenate([small[0], never, small[1], never], axis=0)
    sel = small[2, :, : selected.shape[-1]].astype(jnp.int32)
    place = jnp.stack([ctx // SIDE, ctx % SIDE]).astype(jnp.int32)

    dk, dv, dq_own, dq_far = attend_call(
        sel, place, stats, qd_own, qd_far, key_parts, value_parts, head_dim
    )

    dq_far = swap(dq_far, 1)
    query_grad = jnp.where(
        even, jnp.stack([dq_own, dq_far]), jnp.stack([dq_far, dq_own])
    ).transpose(2, 0, 1, 3)

    dk = reduce_small(reduce_large(*dk, 1, 0), 0, 1)
    dv = reduce_small(reduce_large(*dv, 0, 1), 1, 0)

    grads = jnp.stack([dk, dv]).reshape(2, 4, BLOCK // 4, head_dim)
    a, b, c, d = (grads[:, n] for n in range(4))
    first = jnp.where(even, a, b), jnp.where(even, b, a)
    second = jnp.where(even, c, d), jnp.where(even, d, c)
    near = [jnp.where(lower, first[n], second[n]) for n in range(2)]
    far = [jnp.where(lower, second[n], first[n]) for n in range(2)]
    own = near[0] + swap(far[0].astype(low), 2).astype(full)
    spare = swap(near[1].astype(low), 1).astype(full) + swap(far[1].astype(low), 3).astype(full)
    both = jnp.where(even, jnp.stack([own, spare], 2), jnp.stack([spare, own], 2))
    return (query_grad, both[0], both[1])


def solution(mesh):
    return jax.shard_map(
        local,
        mesh=mesh,
        in_specs=(
            P("ctx", "head", "dp", None),
            P(("ctx", "dp"), "head", None),
            P(("ctx", "dp"), "head", None),
            P("ctx", "head", "dp", None),
            P("ctx", "head", "dp", None),
            P("head", "dp", "ctx"),
            P("ctx", "head", "dp", None),
        ),
        out_specs=(
            P("ctx", "head", "dp", None),
            P(("ctx", "dp"), "head", None),
            P(("ctx", "dp"), "head", None),
        ),
        check_vma=False,
    )
```

```python
import jax
import jax.numpy as jnp
from jax import lax
from jax.experimental import pallas as pl
from jax.experimental.pallas import tpu as pltpu
from jax.sharding import PartitionSpec as P

BLOCK = 256
SIDE = 4


def shifts(rows, columns):
    return [
        (y * SIDE + x, (y + rows) % SIDE * SIDE + (x + columns) % SIDE)
        for y in range(SIDE)
        for x in range(SIDE)
    ]


def move(array, rows, columns):
    return lax.ppermute(array, "ctx", shifts(rows, columns))


def swap(array, bit):
    return lax.ppermute(array, "dp", [(d, d ^ bit) for d in range(4)])


def meet(array, axis, bit):
    stride = SIDE if axis == 0 else 1
    pairs = [(n, (n // stride % SIDE ^ bit) * stride + n - n // stride % SIDE * stride) for n in range(SIDE * SIDE)]
    return lax.ppermute(array, "ctx", pairs)


def gather_small(own, axis):
    pair = jnp.stack([own, meet(own, axis, 1)])
    return jnp.concatenate([pair, meet(pair, axis, 3)])


def reduce_small(terms, axis):
    full, low = jnp.float32, jnp.bfloat16
    pair = terms[:2] + meet(terms[2:].astype(low), axis, 3).astype(full)
    return pair[0] + meet(pair[1].astype(low), axis, 1).astype(full)


def gather_large(own, rows, columns):
    half = own.shape[0] // 2
    before = move(own, rows, columns)
    after = move(own, -rows, -columns)
    far_low = move(before[:half], rows, columns)
    far_high = move(after[half:], -rows, -columns)
    return [own, before, after, far_low, far_high]


def reduce_large(own, before, after, far_low, far_high, rows, columns):
    full, half = jnp.float32, far_low.shape[0]
    low_far = move(far_low, -rows, -columns)
    high_far = move(far_high, rows, columns)
    first = (before[:half].astype(full) + low_far.astype(full)).astype(before.dtype)
    second = (after[half:].astype(full) + high_far.astype(full)).astype(after.dtype)
    before = move(jnp.concatenate([first, before[half:]]), -rows, -columns)
    after = move(jnp.concatenate([after[:half], second]), rows, columns)
    return own.astype(full) + before.astype(full) + after.astype(full)


PARTS = ((0, SIDE), (SIDE, SIDE), (3 * SIDE, SIDE), (2 * SIDE, SIDE // 2), (2 * SIDE + SIDE // 2, SIDE // 2))


def attend(sel, place, stats, qd_own, qd_far, *refs, scale, blocks, pairs):
    count = len(PARTS)
    k_in, v_in = refs[0:count], refs[count : 2 * count]
    k_out, v_out = refs[2 * count : 3 * count], refs[3 * count : 4 * count]
    dq_own, dq_far = refs[4 * count : 4 * count + 2]
    (
        keys,
        vals,
        keys_t,
        q_t,
        do_t,
        p_even,
        s_even,
        p_odd,
        s_odd,
        q,
        do,
        acc_k,
        acc_v,
        dk_low,
        dv_low,
        dq_t,
        item,
        sems,
    ) = refs[4 * count + 2 :]
    half_rows = BLOCK // 2
    half_pairs = pairs // 2
    copies = []
    for n, (first, size) in enumerate(PARTS):
        span = pl.ds(first, size)
        copies.append(pltpu.make_async_copy(k_in[n], keys.at[span], sems.at[n]))
        copies.append(pltpu.make_async_copy(v_in[n], vals.at[span], sems.at[count + n]))
    for copy in copies:
        copy.start()

    row, column, parity = place[0], place[1], place[2]

    def near(distance):
        return distance ^ (distance >> 1)

    def record(at, pair, key_a, value_a, limit_a, key_b, value_b, limit_b):
        for n, word in enumerate((pair, key_a, value_a, limit_a, key_b, value_b, limit_b)):
            item[n, at] = jnp.int32(word)

    def lookup(block):
        y, x = (block >> 2) & 3, block & 3
        key = ((row - y) & 3) * SIDE + near(column ^ x)
        value = ((column - x) & 3) * SIDE + near(row ^ y)
        return key, value

    total = jnp.int32(0)
    for pair in range(pairs):
        for s in range(0, sel.shape[1], 2):
            one, two = sel[pair, s], sel[pair, s + 1]
            first = jnp.int32(0 if s == 0 else BLOCK)
            second = jnp.where(two >= 0, BLOCK, -2 * BLOCK)
            record(total, pair, *lookup(one), first, *lookup(two), second)
            total = total + (one >= 0).astype(jnp.int32)
    record(total, 0, 0, 0, -2 * BLOCK, 0, 0, -2 * BLOCK)

    for part, qd in enumerate((qd_own, qd_far)):
        for g in range(half_pairs):
            q[half_pairs * part + g] = qd[0, g]
            do[half_pairs * part + g] = qd[1, g]
            q_t[half_pairs * part + g] = qd[0, g].T
            do_t[half_pairs * part + g] = qd[1, g].T
    dq_t[...] = jnp.zeros_like(dq_t)

    @pl.loop(0, blocks)
    def _(r):
        acc_k[r] = jnp.zeros(acc_k.shape[1:], jnp.float32)
        acc_v[r] = jnp.zeros(acc_v.shape[1:], jnp.float32)

    for copy in copies:
        copy.wait()

    @pl.loop(0, blocks)
    def _(r):
        for a in range(2):
            keys_t[2 * r + a] = keys[r, a * half_rows : (a + 1) * half_rows].T

    at_row = lax.broadcasted_iota(jnp.int32, (half_rows, BLOCK), 0)
    at_query = lax.broadcasted_iota(jnp.int32, (half_rows, BLOCK), 1)
    quarter = BLOCK // 4
    at_key = at_row + parity * quarter + jnp.where(at_row >= quarter, quarter, 0)
    offset = at_key - at_query

    def both(ref, first, second, head):
        span = pl.ds(pl.multiple_of(head * half_rows, half_rows), half_rows)
        return jnp.concatenate([ref[first, span], ref[second, span]], axis=0)

    def weigh(n, p_buf, s_buf):
        pair, key_a, value_a, limit_a, key_b, value_b, limit_b = (item[w, n] for w in range(7))
        head = (pair >> 1) & 1
        lse = stats[pl.ds(pair, 1), :]
        delta = stats[pl.ds(pair + pairs, 1), :]
        k = both(keys, key_a, key_b, head)
        scores = jnp.dot(k, q_t[pair], preferred_element_type=jnp.float32) * scale
        keep = jnp.concatenate([offset <= limit_a, offset <= limit_b], axis=0)
        probs = jnp.where(keep, jnp.exp(scores - lse), 0.0)
        p_buf[...] = probs.astype(jnp.bfloat16)
        v = both(vals, value_a, value_b, head)
        dprobs = jnp.dot(v, do_t[pair], preferred_element_type=jnp.float32)
        s_buf[...] = (probs * (dprobs - delta) * scale).astype(jnp.bfloat16)

    def spread(n, p_buf, s_buf):
        pair, key_a, value_a, _, key_b, value_b, _ = (item[w, n] for w in range(7))
        head = (pair >> 1) & 1
        span = pl.ds(pl.multiple_of(head * half_rows, half_rows), half_rows)
        dv = jnp.dot(p_buf[...], do[pair], preferred_element_type=jnp.float32)
        acc_v[value_a, span] += dv[:half_rows]
        acc_v[value_b, span] += dv[half_rows:]
        dk = jnp.dot(s_buf[...], q[pair], preferred_element_type=jnp.float32)
        acc_k[key_a, span] += dk[:half_rows]
        acc_k[key_b, span] += dk[half_rows:]
        k_t = jnp.concatenate([keys_t[2 * key_a + head], keys_t[2 * key_b + head]], axis=1)
        dq_t[pair] += jnp.dot(k_t, s_buf[...], preferred_element_type=jnp.float32)

    weigh(0, p_even, s_even)
    steps = (total + 1) >> 1

    @pl.loop(0, steps - 1)
    def _(i):
        weigh(2 * i + 1, p_odd, s_odd)
        spread(2 * i, p_even, s_even)
        weigh(2 * i + 2, p_even, s_even)
        spread(2 * i + 1, p_odd, s_odd)

    last = 2 * steps - 2
    weigh(last + 1, p_odd, s_odd)
    spread(last, p_even, s_even)
    spread(last + 1, p_odd, s_odd)

    @pl.loop(0, blocks)
    def _(r):
        dk_low[r] = acc_k[r].astype(jnp.bfloat16)
        dv_low[r] = acc_v[r].astype(jnp.bfloat16)

    copies = []
    for n, (first, size) in enumerate(PARTS):
        span = pl.ds(first, size)
        copies.append(pltpu.make_async_copy(dk_low.at[span], k_out[n], sems.at[n]))
        copies.append(pltpu.make_async_copy(dv_low.at[span], v_out[n], sems.at[count + n]))
    for copy in copies:
        copy.start()
    for g in range(half_pairs):
        dq_own[g] = dq_t[g].T
        dq_far[g] = dq_t[half_pairs + g].T.astype(jnp.bfloat16)
    for copy in copies:
        copy.wait()


def attend_call(sel, place, stats, qd_own, qd_far, key_parts, value_parts, head_dim):
    blocks = SIDE * SIDE
    vmem = pl.BlockSpec(memory_space=pltpu.VMEM)
    smem = pl.BlockSpec(memory_space=pltpu.SMEM)
    anywhere = pl.BlockSpec(memory_space=pl.ANY)
    low, full = jnp.bfloat16, jnp.float32
    parts = [jax.ShapeDtypeStruct((size, BLOCK, head_dim), low) for _, size in PARTS]
    pairs = sel.shape[0]
    dq_own = jax.ShapeDtypeStruct((pairs // 2, BLOCK, head_dim), full)
    dq_far = jax.ShapeDtypeStruct((pairs // 2, BLOCK, head_dim), low)
    count = len(PARTS)
    outs = pl.pallas_call(
        lambda *refs: attend(*refs, scale=head_dim**-0.5, blocks=blocks, pairs=pairs),
        out_shape=parts * 2 + [dq_own, dq_far],
        in_specs=[smem, smem, vmem, vmem, vmem] + [anywhere] * (2 * count),
        out_specs=[anywhere] * (2 * count) + [vmem] * 2,
        scratch_shapes=[
            pltpu.VMEM((blocks, BLOCK, head_dim), low),
            pltpu.VMEM((blocks, BLOCK, head_dim), low),
            pltpu.VMEM((2 * blocks, head_dim, BLOCK // 2), low),
            pltpu.VMEM((pairs, head_dim, BLOCK), low),
            pltpu.VMEM((pairs, head_dim, BLOCK), low),
            pltpu.VMEM((BLOCK, BLOCK), low),
            pltpu.VMEM((BLOCK, BLOCK), low),
            pltpu.VMEM((BLOCK, BLOCK), low),
            pltpu.VMEM((BLOCK, BLOCK), low),
            pltpu.VMEM((pairs, BLOCK, head_dim), low),
            pltpu.VMEM((pairs, BLOCK, head_dim), low),
            pltpu.VMEM((blocks, BLOCK, head_dim), full),
            pltpu.VMEM((blocks, BLOCK, head_dim), full),
            pltpu.VMEM((blocks, BLOCK, head_dim), low),
            pltpu.VMEM((blocks, BLOCK, head_dim), low),
            pltpu.VMEM((pairs, head_dim, BLOCK), full),
            pltpu.SMEM((8, 40), jnp.int32),
            pltpu.SemaphoreType.DMA((2 * count,)),
        ],
        name="attend",
        compiler_params=pltpu.CompilerParams(vmem_limit_bytes=26 << 20),
        cost_estimate=pl.CostEstimate(
            flops=32 * 5 * 2 * BLOCK * BLOCK * head_dim,
            bytes_accessed=10 << 20,
            transcendentals=32 * BLOCK * BLOCK,
        ),
    )(sel, place, stats, qd_own, qd_far, *key_parts, *value_parts)
    return outs[0:count], outs[count : 2 * count], outs[2 * count], outs[2 * count + 1]


def local(queries, key_rows, value_rows, forward_out, grad_out, logsumexp, selected):
    rows, heads, members, head_dim = queries.shape
    pairs = heads * members
    low, full = jnp.bfloat16, jnp.float32
    ctx, dp = lax.axis_index("ctx"), lax.axis_index("dp")
    lower = dp < 2

    kv = jnp.stack([key_rows, value_rows]).transpose(0, 2, 1, 3)
    far = swap(kv, 2)
    kv = jnp.where(lower, jnp.concatenate([kv, far], 2), jnp.concatenate([far, kv], 2))
    kv = kv.reshape(2, BLOCK, head_dim)

    key_parts = gather_large(gather_small(kv[0], 1), 1, 0)
    value_parts = gather_large(gather_small(kv[1], 0), 0, 1)

    qd_own = jnp.stack([queries, grad_out]).transpose(0, 2, 3, 1, 4).reshape(2, pairs, rows, head_dim)
    qd_far = swap(qd_own, 1)
    delta = jnp.sum(grad_out.astype(full) * forward_out.astype(full), axis=-1).transpose(1, 2, 0)
    ids = jnp.pad(selected[0].astype(full), ((0, 0), (0, 0), (0, BLOCK - selected.shape[-1])))
    small = jnp.stack([logsumexp, delta, ids]).reshape(3, pairs, BLOCK)
    small = jnp.concatenate([small, swap(small, 1)], axis=1)
    stats = small[0:2].reshape(4 * pairs, BLOCK)
    sel = small[2, :, : selected.shape[-1]].astype(jnp.int32)
    place = jnp.stack([ctx // SIDE, ctx % SIDE, dp % 2]).astype(jnp.int32)

    dk, dv, dq_own, dq_far = attend_call(
        sel, place, stats, qd_own, qd_far, key_parts, value_parts, head_dim
    )

    query_grad = (dq_own + swap(dq_far, 1).astype(full)).astype(low)
    query_grad = query_grad.reshape(heads, members, rows, head_dim).transpose(2, 0, 1, 3)

    dk = reduce_small(reduce_large(*dk, 1, 0), 1)
    dv = reduce_small(reduce_large(*dv, 0, 1), 0)

    grads = jnp.stack([dk, dv]).reshape(2, heads, 2, BLOCK // 4, head_dim)
    keep = jnp.where(lower, grads[:, :, 0], grads[:, :, 1])
    send = jnp.where(lower, grads[:, :, 1], grads[:, :, 0]).astype(low)
    grads = (keep + swap(send, 2).astype(full)).transpose(0, 2, 1, 3)
    return (query_grad, grads[0], grads[1])


def solution(mesh):
    return jax.shard_map(
        local,
        mesh=mesh,
        in_specs=(
            P("ctx", "head", "dp", None),
            P(("ctx", "dp"), "head", None),
            P(("ctx", "dp"), "head", None),
            P("ctx", "head", "dp", None),
            P("ctx", "head", "dp", None),
            P("head", "dp", "ctx"),
            P("ctx", "head", "dp", None),
        ),
        out_specs=(
            P("ctx", "head", "dp", None),
            P(("ctx", "dp"), "head", None),
            P(("ctx", "dp"), "head", None),
        ),
        check_vma=False,
    )
```

```python
import jax
import jax.numpy as jnp
from jax import lax
from jax.experimental import pallas as pl
from jax.experimental.pallas import tpu as pltpu
from jax.sharding import PartitionSpec as P

BLOCK = 256
SIDE = 4


def shifts(rows, columns):
    return [
        (y * SIDE + x, (y + rows) % SIDE * SIDE + (x + columns) % SIDE)
        for y in range(SIDE)
        for x in range(SIDE)
    ]


def move(array, rows, columns):
    return lax.ppermute(array, "ctx", shifts(rows, columns))


def swap(array, bit):
    return lax.ppermute(array, "dp", [(d, d ^ bit) for d in range(4)])


def meet(array, axis, bit):
    stride = SIDE if axis == 0 else 1
    pairs = [(n, (n // stride % SIDE ^ bit) * stride + n - n // stride % SIDE * stride) for n in range(SIDE * SIDE)]
    return lax.ppermute(array, "ctx", pairs)


def gather_small(own, axis):
    pair = jnp.stack([own, meet(own, axis, 1)])
    return jnp.concatenate([pair, meet(pair, axis, 3)])


def reduce_small(terms, axis):
    full, low = jnp.float32, jnp.bfloat16
    pair = terms[:2] + meet(terms[2:].astype(low), axis, 3).astype(full)
    return pair[0] + meet(pair[1].astype(low), axis, 1).astype(full)


def gather_large(own, rows, columns):
    before = move(own, rows, columns)
    after = move(own, -rows, -columns)
    return own, before, after, move(before, rows, columns)


def reduce_large(own, before, after, far, rows, columns):
    full = jnp.float32
    after = move(after, rows, columns)
    far, own = lax.optimization_barrier((move(far, -rows, -columns), own))
    before = move((before.astype(full) + far.astype(full)).astype(before.dtype), -rows, -columns)
    return own + before.astype(full) + after.astype(full)


def reduce_small(terms, axis):
    full, low = jnp.float32, jnp.bfloat16
    pair = terms[:2] + meet(terms[2:].astype(low), axis, 3).astype(full)
    return pair[0] + meet(pair[1].astype(low), axis, 1).astype(full)


SETS, WORDS, ROOM = 3, 6, 40
NONE = -2 * BLOCK


def near(distance):
    return distance ^ (distance >> 1)


def plan(sel, place, qd_own, qd_far, table, qd, count, *, pairs):
    for half, part in enumerate((qd_own, qd_far)):
        for g in range(pairs // 2):
            for n in range(2):
                qd[n, half * (pairs // 2) + g] = part[n, g]
    row, column = place[0], place[1]

    def put(c, word, at, value):
        table[(c * WORDS + word) * ROOM + at] = jnp.int32(value)

    for c in range(SETS):
        count[c] = 0
    for pair in range(pairs):
        for s in range(sel.shape[1]):
            block = sel[pair, s]
            y, x = (block >> 2) & 3, block & 3
            if (pair >> 1) & 1 == 0:
                distance, other = (row - y) & 3, near(column ^ x)
            else:
                distance, other = (column - x) & 3, near(row ^ y)
            c = jnp.where(distance == 0, 2, jnp.where(distance == 2, 1, 0))
            at = count[c]
            word = (at & 1) * 2
            put(c, 0, at >> 1, pair)
            put(c, word + 1, at >> 1, other + jnp.where(distance == 3, SIDE, 0))
            put(c, word + 2, at >> 1, 0 if s == 0 else BLOCK)
            count[c] = at + (block >= 0).astype(jnp.int32)
        for c in range(SETS):
            at = count[c]
            put(c, 3, at >> 1, 0)
            put(c, 4, at >> 1, NONE)
            count[c] = at + (at & 1)
    for c in range(SETS):
        at = count[c] >> 1
        for word, value in enumerate((0, 0, NONE, 0, NONE)):
            put(c, word, at, value)
        put(c, 5, 0, at)


def plan_call(sel, place, qd_own, qd_far):
    vmem = pl.BlockSpec(memory_space=pltpu.VMEM)
    smem = pl.BlockSpec(memory_space=pltpu.SMEM)
    pairs = sel.shape[0]
    shape = (2, pairs) + qd_own.shape[2:]
    return pl.pallas_call(
        lambda *refs: plan(*refs, pairs=pairs),
        out_shape=[
            jax.ShapeDtypeStruct((SETS * WORDS * ROOM,), jnp.int32),
            jax.ShapeDtypeStruct(shape, qd_own.dtype),
        ],
        in_specs=[smem, smem, vmem, vmem],
        out_specs=[smem, vmem],
        scratch_shapes=[pltpu.SMEM((SETS + 1,), jnp.int32)],
        name="plan",
        compiler_params=pltpu.CompilerParams(vmem_limit_bytes=8 << 20),
        cost_estimate=pl.CostEstimate(flops=1 << 20, bytes_accessed=4 << 20, transcendentals=0),
    )(sel, place, qd_own, qd_far)


def attend(table, place, stats, qd, *refs, which, parts, scale, pairs, first, final):
    half_rows = BLOCK // 2
    half_pairs = pairs // 2
    low, full = jnp.bfloat16, jnp.float32
    given = refs[: 2 * parts]
    refs = refs[2 * parts :]
    if not first:
        dq_in, refs = refs[0], refs[1:]
    terms, refs = refs[: 2 * parts], refs[2 * parts :]
    if final:
        dq_own, dq_far, dq_t = refs[0], refs[1], refs[-1]
        rows, acc, p_even, s_even, p_odd, s_odd = refs[2:-1]
    else:
        dq_t = refs[0]
        rows, acc, p_even, s_even, p_odd, s_odd = refs[1:]
    blocks = parts * SIDE

    def word(n, at):
        return table[(which * WORDS + n) * ROOM + at]

    total = word(5, 0)
    if first:
        dq_t[...] = jnp.zeros_like(dq_t)
    else:
        dq_t[...] = dq_in[...]

    def slot(head, n, r):
        return (head * blocks + n * SIDE + r) * 2

    for head in range(2):
        for n in range(parts):
            for r in range(SIDE):
                for kv in range(2):
                    at = slot(head, n, r) + kv
                    rows[at] = given[head * parts + n][r, kv * half_rows : (kv + 1) * half_rows]
                    acc[at] = jnp.zeros(acc.shape[1:], full)

    at_row = lax.broadcasted_iota(jnp.int32, (half_rows, BLOCK), 0)
    at_query = lax.broadcasted_iota(jnp.int32, (half_rows, BLOCK), 1)
    quarter = BLOCK // 4
    offset = at_row + place[2] * quarter + jnp.where(at_row >= quarter, quarter, 0) - at_query

    def across(one, two, dim):
        return lax.dot_general(one, two, (((dim,), (dim,)), ((), ())), preferred_element_type=full)

    def item(n):
        pair = word(0, n)
        base = ((pair >> 1) & 1) * blocks
        return pair, (base + word(1, n)) * 2, (base + word(3, n)) * 2

    def weigh(n, p_buf, s_buf):
        pair, one, two = item(n)
        lse = stats[pl.ds(pair, 1), :]
        delta = stats[pl.ds(pair + pairs, 1), :]
        k = jnp.concatenate([rows[one], rows[two]], axis=0)
        scores = across(k, qd[0, pair], 1) * scale
        keep = jnp.concatenate([offset <= word(2, n), offset <= word(4, n)], axis=0)
        probs = jnp.where(keep, jnp.exp(scores - lse), 0.0)
        p_buf[...] = probs.astype(low)
        v = jnp.concatenate([rows[one + 1], rows[two + 1]], axis=0)
        dprobs = across(v, qd[1, pair], 1)
        s_buf[...] = (probs * (dprobs - delta) * scale).astype(low)

    def spread(n, p_buf, s_buf):
        pair, one, two = item(n)
        dv = jnp.dot(p_buf[...], qd[1, pair], preferred_element_type=full)
        acc[one + 1] += dv[:half_rows]
        acc[two + 1] += dv[half_rows:]
        dk = jnp.dot(s_buf[...], qd[0, pair], preferred_element_type=full)
        acc[one] += dk[:half_rows]
        acc[two] += dk[half_rows:]
        k = jnp.concatenate([rows[one], rows[two]], axis=0)
        dq_t[pair] += across(k, s_buf[...], 0)

    @pl.when(total > 0)
    def _():
        weigh(0, p_even, s_even)
        steps = (total + 1) >> 1

        @pl.loop(0, steps - 1)
        def _(i):
            weigh(2 * i + 1, p_odd, s_odd)
            spread(2 * i, p_even, s_even)
            weigh(2 * i + 2, p_even, s_even)
            spread(2 * i + 1, p_odd, s_odd)

        last = 2 * steps - 2
        weigh(last + 1, p_odd, s_odd)
        spread(last, p_even, s_even)
        spread(last + 1, p_odd, s_odd)

    for head in range(2):
        for n in range(parts):
            out = terms[head * parts + n]
            for r in range(SIDE):
                for kv in range(2):
                    out[r, kv * half_rows : (kv + 1) * half_rows] = acc[slot(head, n, r) + kv].astype(
                        out.dtype
                    )
    if final:
        for g in range(half_pairs):
            dq_own[g] = dq_t[g].T
            dq_far[g] = dq_t[half_pairs + g].T.astype(low)


def attend_call(which, table, place, stats, qd, given, dq, final):
    low, full = jnp.bfloat16, jnp.float32
    vmem = pl.BlockSpec(memory_space=pltpu.VMEM)
    smem = pl.BlockSpec(memory_space=pltpu.SMEM)
    parts = len(given) // 2
    pairs, head_dim = qd.shape[1], qd.shape[-1]
    first = dq is None
    share = 8 * parts
    term = jax.ShapeDtypeStruct(given[0].shape, full if final else low)
    dq_shape = jax.ShapeDtypeStruct((pairs, head_dim, BLOCK), full)
    if final:
        dq_outs = [
            jax.ShapeDtypeStruct((pairs // 2, BLOCK, head_dim), full),
            jax.ShapeDtypeStruct((pairs // 2, BLOCK, head_dim), low),
        ]
    else:
        dq_outs = [dq_shape]
    held = parts * SIDE * 4
    square = pltpu.VMEM((BLOCK, BLOCK), low)
    scratch = [
        pltpu.VMEM((held, BLOCK // 2, head_dim), low),
        pltpu.VMEM((held, BLOCK // 2, head_dim), full),
        square,
        square,
        square,
        square,
    ]
    if final:
        scratch.append(pltpu.VMEM((pairs, head_dim, BLOCK), full))
    operands = (table, place, stats, qd, *given) + (() if first else (dq,))
    outs = pl.pallas_call(
        lambda *refs: attend(
            *refs,
            which=which,
            parts=parts,
            scale=head_dim**-0.5,
            pairs=pairs,
            first=first,
            final=final,
        ),
        out_shape=[term] * len(given) + dq_outs,
        in_specs=[smem, smem] + [vmem] * (len(operands) - 2),
        out_specs=[vmem] * (len(given) + len(dq_outs)),
        scratch_shapes=scratch,
        name=f"attend_{which}",
        compiler_params=pltpu.CompilerParams(vmem_limit_bytes=20 << 20),
        cost_estimate=pl.CostEstimate(
            flops=share * 5 * 2 * BLOCK * BLOCK * head_dim,
            bytes_accessed=(2 * parts + 4) << 20,
            transcendentals=share * BLOCK * BLOCK,
        ),
    )(*operands)
    return outs[: len(given)], outs[len(given) :]


def local(queries, key_rows, value_rows, forward_out, grad_out, logsumexp, selected):
    rows, heads, members, head_dim = queries.shape
    pairs = heads * members
    low, full = jnp.bfloat16, jnp.float32
    ctx, dp = lax.axis_index("ctx"), lax.axis_index("dp")
    lower = dp < 2

    kv = jnp.stack([key_rows, value_rows]).transpose(2, 0, 1, 3)
    far = swap(kv, 2)
    kv = jnp.where(lower, jnp.concatenate([kv, far], 2), jnp.concatenate([far, kv], 2))
    kv = kv.reshape(heads, BLOCK, head_dim)

    qd_own = jnp.stack([queries, grad_out]).transpose(0, 2, 3, 1, 4).reshape(2, pairs, rows, head_dim)
    qd_own, kv = lax.optimization_barrier((qd_own, kv))
    qd_far = swap(qd_own, 1)

    own_0, before_0, after_0, far_0 = gather_large(gather_small(kv[0], 1), 1, 0)
    own_1, before_1, after_1, far_1 = gather_large(gather_small(kv[1], 0), 0, 1)

    delta = jnp.sum(grad_out.astype(full) * forward_out.astype(full), axis=-1).transpose(1, 2, 0)
    ids = jnp.pad(selected[0].astype(full), ((0, 0), (0, 0), (0, BLOCK - selected.shape[-1])))
    small = jnp.stack([logsumexp, delta, ids]).reshape(3, pairs, BLOCK)
    small = jnp.concatenate([small, swap(small, 1)], axis=1)
    stats = small[0:2].reshape(4 * pairs, BLOCK)
    sel = small[2, :, : selected.shape[-1]].astype(jnp.int32)
    place = jnp.stack([ctx // SIDE, ctx % SIDE, dp % 2]).astype(jnp.int32)

    table, qd = plan_call(sel, place, qd_own, qd_far)
    shared = (table, place, stats, qd)
    near_parts = (before_0, after_0, before_1, after_1)
    (before_0, after_0, before_1, after_1), (dq,) = attend_call(0, *shared, near_parts, None, False)
    (far_0, far_1), (dq,) = attend_call(1, *shared, (far_0, far_1), dq, False)
    (own_0, own_1), (dq_own, dq_far) = attend_call(2, *shared, (own_0, own_1), dq, True)

    query_grad = (dq_own + swap(dq_far, 1).astype(full)).astype(low)
    query_grad = query_grad.reshape(heads, members, rows, head_dim).transpose(2, 0, 1, 3)

    grad_0 = reduce_small(reduce_large(own_0, before_0, after_0, far_0, 1, 0), 1)
    grad_1 = reduce_small(reduce_large(own_1, before_1, after_1, far_1, 0, 1), 0)

    grads = jnp.stack([grad_0, grad_1]).reshape(heads, 2, 2, BLOCK // 4, head_dim)
    keep = jnp.where(lower, grads[:, :, 0], grads[:, :, 1])
    send = jnp.where(lower, grads[:, :, 1], grads[:, :, 0]).astype(low)
    grads = (keep + swap(send, 2).astype(full)).transpose(1, 2, 0, 3)
    return (query_grad, grads[0], grads[1])


def solution(mesh):
    return jax.shard_map(
        local,
        mesh=mesh,
        in_specs=(
            P("ctx", "head", "dp", None),
            P(("ctx", "dp"), "head", None),
            P(("ctx", "dp"), "head", None),
            P("ctx", "head", "dp", None),
            P("ctx", "head", "dp", None),
            P("head", "dp", "ctx"),
            P("ctx", "head", "dp", None),
        ),
        out_specs=(
            P("ctx", "head", "dp", None),
            P(("ctx", "dp"), "head", None),
            P(("ctx", "dp"), "head", None),
        ),
        check_vma=False,
    )
```

```python
import jax
import jax.numpy as jnp
from jax import lax
from jax.experimental import pallas as pl
from jax.experimental.pallas import tpu as pltpu
from jax.sharding import PartitionSpec as P


BLOCK = 256
SIDE = 4


def shifts(rows, columns):
    return [
        (y * SIDE + x, (y + rows) % SIDE * SIDE + (x + columns) % SIDE)
        for y in range(SIDE)
        for x in range(SIDE)
    ]


def move(array, rows, columns):
    return lax.ppermute(array, "ctx", shifts(rows, columns))


def swap(array, bit):
    return lax.ppermute(array, "dp", [(d, d ^ bit) for d in range(4)])


def gather_small(own, rows, columns):
    before = move(own, rows, columns)
    after = move(own, -rows, -columns)
    far = move(own, 2 * rows, 2 * columns)
    return jnp.stack([own, before, far, after])


def gather_large(own, rows, columns):
    before = move(own, rows, columns)
    after = move(own, -rows, -columns)
    far = move(before, rows, columns)
    return own, before, after, far


def reduce_large(own, before, after, far, rows, columns):
    full = jnp.float32
    after = move(after, rows, columns)
    far, own = lax.optimization_barrier((move(far, -rows, -columns), own))
    before = move((before.astype(full) + far.astype(full)).astype(before.dtype), -rows, -columns)
    return own + before.astype(full) + after.astype(full)


def reduce_small(terms, rows, columns):
    full, low = jnp.float32, terms.astype(jnp.bfloat16)
    far = move(low[2], -2 * rows, -2 * columns)
    before = move(low[1], -rows, -columns)
    after = move(low[3], rows, columns)
    return terms[0] + far.astype(full) + before.astype(full) + after.astype(full)


SETS, WORDS, ROOM = 3, 6, 40
NONE = -2 * BLOCK


def plan(sel, place, qd_own, qd_far, table, qd, count, *, pairs):
    for half, part in enumerate((qd_own, qd_far)):
        for g in range(pairs // 2):
            for n in range(2):
                qd[n, half * (pairs // 2) + g] = part[n, g]
    row, column = place[0], place[1]

    def put(c, word, at, value):
        table[(c * WORDS + word) * ROOM + at] = jnp.int32(value)

    for c in range(SETS):
        count[c] = 0
    for pair in range(pairs):
        for s in range(sel.shape[1]):
            block = sel[pair, s]
            y, x = (block >> 2) & 3, block & 3
            if (pair >> 1) & 1 == 0:
                distance, other = (row - y) & 3, (column - x) & 3
            else:
                distance, other = (column - x) & 3, (row - y) & 3
            c = jnp.where(distance == 0, 2, jnp.where(distance == 2, 1, 0))
            at = count[c]
            word = (at & 1) * 2
            put(c, 0, at >> 1, pair)
            put(c, word + 1, at >> 1, other + jnp.where(distance == 3, SIDE, 0))
            put(c, word + 2, at >> 1, 0 if s == 0 else BLOCK)
            count[c] = at + (block >= 0).astype(jnp.int32)
        for c in range(SETS):
            at = count[c]
            put(c, 3, at >> 1, 0)
            put(c, 4, at >> 1, NONE)
            count[c] = at + (at & 1)
    for c in range(SETS):
        at = count[c] >> 1
        for word, value in enumerate((0, 0, NONE, 0, NONE)):
            put(c, word, at, value)
        put(c, 5, 0, at)


def plan_call(sel, place, qd_own, qd_far):
    vmem = pl.BlockSpec(memory_space=pltpu.VMEM)
    smem = pl.BlockSpec(memory_space=pltpu.SMEM)
    pairs = sel.shape[0]
    shape = (2, pairs) + qd_own.shape[2:]
    return pl.pallas_call(
        lambda *refs: plan(*refs, pairs=pairs),
        out_shape=[
            jax.ShapeDtypeStruct((SETS * WORDS * ROOM,), jnp.int32),
            jax.ShapeDtypeStruct(shape, qd_own.dtype),
        ],
        in_specs=[smem, smem, vmem, vmem],
        out_specs=[smem, vmem],
        scratch_shapes=[pltpu.SMEM((SETS + 1,), jnp.int32)],
        name="plan",
        compiler_params=pltpu.CompilerParams(vmem_limit_bytes=8 << 20),
        cost_estimate=pl.CostEstimate(flops=1 << 20, bytes_accessed=4 << 20, transcendentals=0),
    )(sel, place, qd_own, qd_far)


def attend(table, place, stats, qd, *refs, which, parts, scale, pairs, first, final):
    half_rows = BLOCK // 2
    half_pairs = pairs // 2
    low, full = jnp.bfloat16, jnp.float32
    given = refs[: 2 * parts]
    refs = refs[2 * parts :]
    if not first:
        dq_in, refs = refs[0], refs[1:]
    terms, refs = refs[: 2 * parts], refs[2 * parts :]
    if final:
        dq_own, dq_far, dq_t = refs[0], refs[1], refs[-1]
        rows, acc, p_even, s_even, p_odd, s_odd = refs[2:-1]
    else:
        dq_t = refs[0]
        rows, acc, p_even, s_even, p_odd, s_odd = refs[1:]
    blocks = parts * SIDE

    def word(n, at):
        return table[(which * WORDS + n) * ROOM + at]

    total = word(5, 0)
    if first:
        dq_t[...] = jnp.zeros_like(dq_t)
    else:
        dq_t[...] = dq_in[...]

    def slot(head, n, r):
        return (head * blocks + n * SIDE + r) * 2

    for head in range(2):
        for n in range(parts):
            for r in range(SIDE):
                for kv in range(2):
                    at = slot(head, n, r) + kv
                    rows[at] = given[head * parts + n][r, kv * half_rows : (kv + 1) * half_rows]
                    acc[at] = jnp.zeros(acc.shape[1:], full)

    at_row = lax.broadcasted_iota(jnp.int32, (half_rows, BLOCK), 0)
    at_query = lax.broadcasted_iota(jnp.int32, (half_rows, BLOCK), 1)
    quarter = BLOCK // 4
    offset = at_row + place[2] * quarter + jnp.where(at_row >= quarter, quarter, 0) - at_query

    def across(one, two, dim):
        return lax.dot_general(one, two, (((dim,), (dim,)), ((), ())), preferred_element_type=full)

    def item(n):
        pair = word(0, n)
        base = ((pair >> 1) & 1) * blocks
        return pair, (base + word(1, n)) * 2, (base + word(3, n)) * 2

    def weigh(n, p_buf, s_buf):
        pair, one, two = item(n)
        lse = stats[pl.ds(pair, 1), :]
        delta = stats[pl.ds(pair + pairs, 1), :]
        k = jnp.concatenate([rows[one], rows[two]], axis=0)
        scores = across(k, qd[0, pair], 1) * scale
        keep = jnp.concatenate([offset <= word(2, n), offset <= word(4, n)], axis=0)
        probs = jnp.where(keep, jnp.exp(scores - lse), 0.0)
        p_buf[...] = probs.astype(low)
        v = jnp.concatenate([rows[one + 1], rows[two + 1]], axis=0)
        dprobs = across(v, qd[1, pair], 1)
        s_buf[...] = (probs * (dprobs - delta) * scale).astype(low)

    def spread(n, p_buf, s_buf):
        pair, one, two = item(n)
        dv = jnp.dot(p_buf[...], qd[1, pair], preferred_element_type=full)
        acc[one + 1] += dv[:half_rows]
        acc[two + 1] += dv[half_rows:]
        dk = jnp.dot(s_buf[...], qd[0, pair], preferred_element_type=full)
        acc[one] += dk[:half_rows]
        acc[two] += dk[half_rows:]
        k = jnp.concatenate([rows[one], rows[two]], axis=0)
        dq_t[pair] += across(k, s_buf[...], 0)

    @pl.when(total > 0)
    def _():
        weigh(0, p_even, s_even)
        steps = (total + 1) >> 1

        @pl.loop(0, steps - 1)
        def _(i):
            weigh(2 * i + 1, p_odd, s_odd)
            spread(2 * i, p_even, s_even)
            weigh(2 * i + 2, p_even, s_even)
            spread(2 * i + 1, p_odd, s_odd)

        last = 2 * steps - 2
        weigh(last + 1, p_odd, s_odd)
        spread(last, p_even, s_even)
        spread(last + 1, p_odd, s_odd)

    for head in range(2):
        for n in range(parts):
            out = terms[head * parts + n]
            for r in range(SIDE):
                for kv in range(2):
                    out[r, kv * half_rows : (kv + 1) * half_rows] = acc[slot(head, n, r) + kv].astype(
                        out.dtype
                    )
    if final:
        for g in range(half_pairs):
            dq_own[g] = dq_t[g].T
            dq_far[g] = dq_t[half_pairs + g].T.astype(low)


def attend_call(which, table, place, stats, qd, given, dq, final):
    low, full = jnp.bfloat16, jnp.float32
    vmem = pl.BlockSpec(memory_space=pltpu.VMEM)
    smem = pl.BlockSpec(memory_space=pltpu.SMEM)
    parts = len(given) // 2
    pairs, head_dim = qd.shape[1], qd.shape[-1]
    first = dq is None
    share = 8 * parts
    term = jax.ShapeDtypeStruct(given[0].shape, full if final else low)
    dq_shape = jax.ShapeDtypeStruct((pairs, head_dim, BLOCK), full)
    if final:
        dq_outs = [
            jax.ShapeDtypeStruct((pairs // 2, BLOCK, head_dim), full),
            jax.ShapeDtypeStruct((pairs // 2, BLOCK, head_dim), low),
        ]
    else:
        dq_outs = [dq_shape]
    held = parts * SIDE * 4
    square = pltpu.VMEM((BLOCK, BLOCK), low)
    scratch = [
        pltpu.VMEM((held, BLOCK // 2, head_dim), low),
        pltpu.VMEM((held, BLOCK // 2, head_dim), full),
        square,
        square,
        square,
        square,
    ]
    if final:
        scratch.append(pltpu.VMEM((pairs, head_dim, BLOCK), full))
    operands = (table, place, stats, qd, *given) + (() if first else (dq,))
    outs = pl.pallas_call(
        lambda *refs: attend(
            *refs,
            which=which,
            parts=parts,
            scale=head_dim**-0.5,
            pairs=pairs,
            first=first,
            final=final,
        ),
        out_shape=[term] * len(given) + dq_outs,
        in_specs=[smem, smem] + [vmem] * (len(operands) - 2),
        out_specs=[vmem] * (len(given) + len(dq_outs)),
        scratch_shapes=scratch,
        compiler_params=pltpu.CompilerParams(vmem_limit_bytes=20 << 20),
        cost_estimate=pl.CostEstimate(
            flops=share * 5 * 2 * BLOCK * BLOCK * head_dim,
            bytes_accessed=(2 * parts + 4) << 20,
            transcendentals=share * BLOCK * BLOCK,
        ),
    )(*operands)
    return outs[: len(given)], outs[len(given) :]


def step(queries, key_rows, value_rows, forward_out, grad_out, logsumexp, selected):
    rows, heads, members, head_dim = queries.shape
    pairs = heads * members
    low, full = jnp.bfloat16, jnp.float32
    ctx, dp = lax.axis_index("ctx"), lax.axis_index("dp")
    lower = dp < 2

    kv = jnp.stack([key_rows, value_rows]).transpose(2, 0, 1, 3)
    far = swap(kv, 2)
    kv = jnp.where(lower, jnp.concatenate([kv, far], 2), jnp.concatenate([far, kv], 2))
    kv = kv.reshape(heads, BLOCK, head_dim)

    qd_own = jnp.stack([queries, grad_out]).transpose(0, 2, 3, 1, 4).reshape(2, pairs, rows, head_dim)
    qd_far = swap(qd_own, 1)

    own_0, before_0, after_0, far_0 = gather_large(gather_small(kv[0], 0, 1), 1, 0)
    own_1, before_1, after_1, far_1 = gather_large(gather_small(kv[1], 1, 0), 0, 1)

    delta = jnp.sum(grad_out.astype(full) * forward_out.astype(full), axis=-1).transpose(1, 2, 0)
    ids = jnp.pad(selected[0].astype(full), ((0, 0), (0, 0), (0, BLOCK - selected.shape[-1])))
    small = jnp.stack([logsumexp, delta, ids]).reshape(3, pairs, BLOCK)
    small_far = swap(small, 1)
    small = jnp.concatenate([small, small_far], axis=1)
    stats = small[0:2].reshape(4 * pairs, BLOCK)
    sel = small[2, :, : selected.shape[-1]].astype(jnp.int32)
    place = jnp.stack([ctx // SIDE, ctx % SIDE, dp % 2]).astype(jnp.int32)

    table, qd = plan_call(sel, place, qd_own, qd_far)
    shared = (table, place, stats, qd)
    near_parts = (before_0, after_0, before_1, after_1)
    (before_0, after_0, before_1, after_1), (dq,) = attend_call(0, *shared, near_parts, None, False)
    (far_0, far_1), (dq,) = attend_call(1, *shared, (far_0, far_1), dq, False)
    (own_0, own_1), (dq_own, dq_far) = attend_call(2, *shared, (own_0, own_1), dq, True)

    query_grad = (dq_own + swap(dq_far, 1).astype(full)).astype(low)
    query_grad = query_grad.reshape(heads, members, rows, head_dim).transpose(2, 0, 1, 3)

    grad_0 = reduce_small(reduce_large(own_0, before_0, after_0, far_0, 1, 0), 0, 1)
    grad_1 = reduce_small(reduce_large(own_1, before_1, after_1, far_1, 0, 1), 1, 0)

    grads = jnp.stack([grad_0, grad_1]).reshape(heads, 2, 2, BLOCK // 4, head_dim)
    keep = jnp.where(lower, grads[:, :, 0], grads[:, :, 1])
    send = jnp.where(lower, grads[:, :, 1], grads[:, :, 0]).astype(low)
    grads = (keep + swap(send, 2).astype(full)).transpose(1, 2, 0, 3)
    return (query_grad, grads[0], grads[1])


def solution(mesh):
    return jax.shard_map(
        step,
        mesh=mesh,
        in_specs=(
            P("ctx", "head", "dp", None),
            P(("ctx", "dp"), "head", None),
            P(("ctx", "dp"), "head", None),
            P("ctx", "head", "dp", None),
            P("ctx", "head", "dp", None),
            P("head", "dp", "ctx"),
            P("ctx", "head", "dp", None),
        ),
        out_specs=(
            P("ctx", "head", "dp", None),
            P(("ctx", "dp"), "head", None),
            P(("ctx", "dp"), "head", None),
        ),
        check_vma=False,
    )
```

```python
import jax
import jax.numpy as jnp
from jax import lax
from jax.experimental import pallas as pl
from jax.experimental.pallas import tpu as pltpu
from jax.sharding import PartitionSpec as P


BLOCK = 256
SIDE = 4


def move(array, rows, columns, kept=range(SIDE)):
    pairs = [
        (y * SIDE + x, (y + rows) % SIDE * SIDE + (x + columns) % SIDE)
        for y in kept
        for x in range(SIDE)
    ]
    return lax.ppermute(array, "ctx", pairs)


def senders(rows, distance, lead=0):
    every = range(SIDE)
    return [y for y in every if 0 <= y - lead < SIDE - distance] if rows else every


def returners(rows, distance):
    every = range(SIDE)
    return [y for y in every if y >= distance] if rows else every


def swap(array, bit):
    return lax.ppermute(array, "dp", [(d, d ^ bit) for d in range(4)])


def gather_small(own, rows, columns):
    before = move(own, rows, columns, senders(rows, 1))
    after = move(own, -rows, -columns, senders(rows, 3))
    far = move(own, 2 * rows, 2 * columns, senders(rows, 2))
    return jnp.stack([own, before, far, after])


def gather_large(own, rows, columns):
    before = move(own, rows, columns, senders(rows, 1))
    after = move(own, -rows, -columns, senders(rows, 3))
    far = move(before, rows, columns, senders(rows, 2, 1))
    return own, before, after, far


def reduce_large(own, before, after, far, rows, columns):
    full = jnp.float32
    after = move(after, rows, columns, returners(rows, 3))
    far = move(far, -rows, -columns, returners(rows, 2))
    far, own = lax.optimization_barrier((far, own))
    near = (before.astype(full) + far.astype(full)).astype(before.dtype)
    before = move(near, -rows, -columns, returners(rows, 1))
    return own + before.astype(full) + after.astype(full)


def reduce_small(terms, rows, columns):
    full, low = jnp.float32, terms.astype(jnp.bfloat16)
    far = move(low[2], -2 * rows, -2 * columns, returners(rows, 2))
    before = move(low[1], -rows, -columns, returners(rows, 1))
    after = move(low[3], rows, columns, returners(rows, 3))
    return terms[0] + far.astype(full) + before.astype(full) + after.astype(full)


SETS, WORDS, ROOM = 3, 6, 40
NONE = -2 * BLOCK


def plan(sel, place, qd_own, qd_far, table, qd, count, *, pairs):
    for half, part in enumerate((qd_own, qd_far)):
        for g in range(pairs // 2):
            for n in range(2):
                qd[n, half * (pairs // 2) + g] = part[n, g]
    row, column = place[0], place[1]

    def put(c, word, at, value):
        table[(c * WORDS + word) * ROOM + at] = jnp.int32(value)

    for c in range(SETS):
        count[c] = 0
    for pair in range(pairs):
        for s in range(sel.shape[1]):
            block = sel[pair, s]
            y, x = (block >> 2) & 3, block & 3
            if (pair >> 1) & 1 == 0:
                distance, other = (row - y) & 3, (column - x) & 3
            else:
                distance, other = (column - x) & 3, (row - y) & 3
            c = jnp.where(distance == 0, 2, jnp.where(distance == 2, 1, 0))
            at = count[c]
            word = (at & 1) * 2
            put(c, 0, at >> 1, pair)
            put(c, word + 1, at >> 1, other + jnp.where(distance == 3, SIDE, 0))
            put(c, word + 2, at >> 1, 0 if s == 0 else BLOCK)
            count[c] = at + (block >= 0).astype(jnp.int32)
        for c in range(SETS):
            at = count[c]
            put(c, 3, at >> 1, 0)
            put(c, 4, at >> 1, NONE)
            count[c] = at + (at & 1)
    for c in range(SETS):
        at = count[c] >> 1
        for word, value in enumerate((0, 0, NONE, 0, NONE)):
            put(c, word, at, value)
        put(c, 5, 0, at)


def plan_call(sel, place, qd_own, qd_far):
    vmem = pl.BlockSpec(memory_space=pltpu.VMEM)
    smem = pl.BlockSpec(memory_space=pltpu.SMEM)
    pairs = sel.shape[0]
    shape = (2, pairs) + qd_own.shape[2:]
    return pl.pallas_call(
        lambda *refs: plan(*refs, pairs=pairs),
        out_shape=[
            jax.ShapeDtypeStruct((SETS * WORDS * ROOM,), jnp.int32),
            jax.ShapeDtypeStruct(shape, qd_own.dtype),
        ],
        in_specs=[smem, smem, vmem, vmem],
        out_specs=[smem, vmem],
        scratch_shapes=[pltpu.SMEM((SETS + 1,), jnp.int32)],
        name="plan",
        compiler_params=pltpu.CompilerParams(vmem_limit_bytes=8 << 20),
        cost_estimate=pl.CostEstimate(flops=1 << 20, bytes_accessed=4 << 20, transcendentals=0),
    )(sel, place, qd_own, qd_far)


def attend(table, place, stats, qd, *refs, which, parts, scale, pairs, first, final):
    half_rows = BLOCK // 2
    half_pairs = pairs // 2
    low, full = jnp.bfloat16, jnp.float32
    given = refs[: 2 * parts]
    refs = refs[2 * parts :]
    if not first:
        dq_in, refs = refs[0], refs[1:]
    terms, refs = refs[: 2 * parts], refs[2 * parts :]
    if final:
        dq_own, dq_far, dq_t = refs[0], refs[1], refs[-1]
        rows, acc, p_even, s_even, p_odd, s_odd = refs[2:-1]
    else:
        dq_t = refs[0]
        rows, acc, p_even, s_even, p_odd, s_odd = refs[1:]
    blocks = parts * SIDE

    def word(n, at):
        return table[(which * WORDS + n) * ROOM + at]

    total = word(5, 0)
    if first:
        dq_t[...] = jnp.zeros_like(dq_t)
    else:
        dq_t[...] = dq_in[...]

    def slot(head, n, r):
        return (head * blocks + n * SIDE + r) * 2

    for head in range(2):
        for n in range(parts):
            for r in range(SIDE):
                for kv in range(2):
                    at = slot(head, n, r) + kv
                    rows[at] = given[head * parts + n][r, kv * half_rows : (kv + 1) * half_rows]
                    acc[at] = jnp.zeros(acc.shape[1:], full)

    at_row = lax.broadcasted_iota(jnp.int32, (half_rows, BLOCK), 0)
    at_query = lax.broadcasted_iota(jnp.int32, (half_rows, BLOCK), 1)
    quarter = BLOCK // 4
    offset = at_row + place[2] * quarter + jnp.where(at_row >= quarter, quarter, 0) - at_query

    def across(one, two, dim):
        return lax.dot_general(one, two, (((dim,), (dim,)), ((), ())), preferred_element_type=full)

    def item(n):
        pair = word(0, n)
        base = ((pair >> 1) & 1) * blocks
        return pair, (base + word(1, n)) * 2, (base + word(3, n)) * 2

    def weigh(n, p_buf, s_buf):
        pair, one, two = item(n)
        lse = stats[pl.ds(pair, 1), :]
        delta = stats[pl.ds(pair + pairs, 1), :]
        k = jnp.concatenate([rows[one], rows[two]], axis=0)
        scores = across(k, qd[0, pair], 1) * scale
        keep = jnp.concatenate([offset <= word(2, n), offset <= word(4, n)], axis=0)
        probs = jnp.where(keep, jnp.exp(scores - lse), 0.0)
        p_buf[...] = probs.astype(low)
        v = jnp.concatenate([rows[one + 1], rows[two + 1]], axis=0)
        dprobs = across(v, qd[1, pair], 1)
        s_buf[...] = (probs * (dprobs - delta) * scale).astype(low)

    def spread(n, p_buf, s_buf):
        pair, one, two = item(n)
        dv = jnp.dot(p_buf[...], qd[1, pair], preferred_element_type=full)
        acc[one + 1] += dv[:half_rows]
        acc[two + 1] += dv[half_rows:]
        dk = jnp.dot(s_buf[...], qd[0, pair], preferred_element_type=full)
        acc[one] += dk[:half_rows]
        acc[two] += dk[half_rows:]
        k = jnp.concatenate([rows[one], rows[two]], axis=0)
        dq_t[pair] += across(k, s_buf[...], 0)

    @pl.when(total > 0)
    def _():
        weigh(0, p_even, s_even)
        steps = (total + 1) >> 1

        @pl.loop(0, steps - 1)
        def _(i):
            weigh(2 * i + 1, p_odd, s_odd)
            spread(2 * i, p_even, s_even)
            weigh(2 * i + 2, p_even, s_even)
            spread(2 * i + 1, p_odd, s_odd)

        last = 2 * steps - 2
        weigh(last + 1, p_odd, s_odd)
        spread(last, p_even, s_even)
        spread(last + 1, p_odd, s_odd)

    for head in range(2):
        for n in range(parts):
            out = terms[head * parts + n]
            for r in range(SIDE):
                for kv in range(2):
                    out[r, kv * half_rows : (kv + 1) * half_rows] = acc[slot(head, n, r) + kv].astype(
                        out.dtype
                    )
    if final:
        for g in range(half_pairs):
            dq_own[g] = dq_t[g].T
            dq_far[g] = dq_t[half_pairs + g].T.astype(low)


def attend_call(which, table, place, stats, qd, given, dq, final):
    low, full = jnp.bfloat16, jnp.float32
    vmem = pl.BlockSpec(memory_space=pltpu.VMEM)
    smem = pl.BlockSpec(memory_space=pltpu.SMEM)
    parts = len(given) // 2
    pairs, head_dim = qd.shape[1], qd.shape[-1]
    first = dq is None
    share = 8 * parts
    term = jax.ShapeDtypeStruct(given[0].shape, full if final else low)
    dq_shape = jax.ShapeDtypeStruct((pairs, head_dim, BLOCK), full)
    if final:
        dq_outs = [
            jax.ShapeDtypeStruct((pairs // 2, BLOCK, head_dim), full),
            jax.ShapeDtypeStruct((pairs // 2, BLOCK, head_dim), low),
        ]
    else:
        dq_outs = [dq_shape]
    held = parts * SIDE * 4
    square = pltpu.VMEM((BLOCK, BLOCK), low)
    scratch = [
        pltpu.VMEM((held, BLOCK // 2, head_dim), low),
        pltpu.VMEM((held, BLOCK // 2, head_dim), full),
        square,
        square,
        square,
        square,
    ]
    if final:
        scratch.append(pltpu.VMEM((pairs, head_dim, BLOCK), full))
    operands = (table, place, stats, qd, *given) + (() if first else (dq,))
    outs = pl.pallas_call(
        lambda *refs: attend(
            *refs,
            which=which,
            parts=parts,
            scale=head_dim**-0.5,
            pairs=pairs,
            first=first,
            final=final,
        ),
        out_shape=[term] * len(given) + dq_outs,
        in_specs=[smem, smem] + [vmem] * (len(operands) - 2),
        out_specs=[vmem] * (len(given) + len(dq_outs)),
        scratch_shapes=scratch,
        compiler_params=pltpu.CompilerParams(vmem_limit_bytes=20 << 20),
        cost_estimate=pl.CostEstimate(
            flops=share * 5 * 2 * BLOCK * BLOCK * head_dim,
            bytes_accessed=(2 * parts + 4) << 20,
            transcendentals=share * BLOCK * BLOCK,
        ),
    )(*operands)
    return outs[: len(given)], outs[len(given) :]


def step(queries, key_rows, value_rows, forward_out, grad_out, logsumexp, selected):
    rows, heads, members, head_dim = queries.shape
    pairs = heads * members
    low, full = jnp.bfloat16, jnp.float32
    ctx, dp = lax.axis_index("ctx"), lax.axis_index("dp")
    lower = dp < 2

    kv = jnp.stack([key_rows, value_rows]).transpose(2, 0, 1, 3)
    far = swap(kv, 2)
    kv = jnp.where(lower, jnp.concatenate([kv, far], 2), jnp.concatenate([far, kv], 2))
    kv = kv.reshape(heads, BLOCK, head_dim)

    qd_own = jnp.stack([queries, grad_out]).transpose(0, 2, 3, 1, 4).reshape(2, pairs, rows, head_dim)
    qd_far = swap(qd_own, 1)

    own_0, before_0, after_0, far_0 = gather_large(gather_small(kv[0], 0, 1), 1, 0)
    own_1, before_1, after_1, far_1 = gather_large(gather_small(kv[1], 1, 0), 0, 1)

    delta = jnp.sum(grad_out.astype(full) * forward_out.astype(full), axis=-1)
    delta = delta.transpose(1, 2, 0)
    ids = jnp.pad(selected[0].astype(full), ((0, 0), (0, 0), (0, BLOCK - selected.shape[-1])))
    small = jnp.stack([logsumexp, delta, ids]).reshape(3, pairs, BLOCK)
    small_far = swap(small, 1)
    small = jnp.concatenate([small, small_far], axis=1)
    stats = small[0:2].reshape(4 * pairs, BLOCK)
    sel = small[2, :, : selected.shape[-1]].astype(jnp.int32)
    place = jnp.stack([ctx // SIDE, ctx % SIDE, dp % 2]).astype(jnp.int32)

    table, qd = plan_call(sel, place, qd_own, qd_far)
    shared = (table, place, stats, qd)
    near_parts = (before_0, after_0, before_1, after_1)
    (before_0, after_0, before_1, after_1), (dq,) = attend_call(0, *shared, near_parts, None, False)
    (far_0, far_1), (dq,) = attend_call(1, *shared, (far_0, far_1), dq, False)
    (own_0, own_1), (dq_own, dq_far) = attend_call(2, *shared, (own_0, own_1), dq, True)

    query_grad = (dq_own + swap(dq_far, 1).astype(full)).astype(low)
    query_grad = query_grad.reshape(heads, members, rows, head_dim).transpose(2, 0, 1, 3)

    grad_0 = reduce_small(reduce_large(own_0, before_0, after_0, far_0, 1, 0), 0, 1)
    grad_1 = reduce_small(reduce_large(own_1, before_1, after_1, far_1, 0, 1), 1, 0)

    grads = jnp.stack([grad_0, grad_1]).reshape(heads, 2, 2, BLOCK // 4, head_dim)
    keep = jnp.where(lower, grads[:, :, 0], grads[:, :, 1])
    send = jnp.where(lower, grads[:, :, 1], grads[:, :, 0]).astype(low)
    grads = (keep + swap(send, 2).astype(full)).transpose(1, 2, 0, 3)
    return (query_grad, grads[0], grads[1])


def solution(mesh):
    return jax.shard_map(
        step,
        mesh=mesh,
        in_specs=(
            P("ctx", "head", "dp", None),
            P(("ctx", "dp"), "head", None),
            P(("ctx", "dp"), "head", None),
            P("ctx", "head", "dp", None),
            P("ctx", "head", "dp", None),
            P("head", "dp", "ctx"),
            P("ctx", "head", "dp", None),
        ),
        out_specs=(
            P("ctx", "head", "dp", None),
            P(("ctx", "dp"), "head", None),
            P(("ctx", "dp"), "head", None),
        ),
        check_vma=False,
    )
```

```python
import jax
import jax.numpy as jnp
from jax import lax
from jax.experimental import pallas as pl
from jax.experimental.pallas import tpu as pltpu
from jax.sharding import PartitionSpec as P


BLOCK = 256
SIDE = 4


def shifts(rows, columns):
    return [
        (y * SIDE + x, (y + rows) % SIDE * SIDE + (x + columns) % SIDE)
        for y in range(SIDE)
        for x in range(SIDE)
    ]


def move(array, rows, columns):
    return lax.ppermute(array, "ctx", shifts(rows, columns))


def swap(array, bit):
    return lax.ppermute(array, "dp", [(d, d ^ bit) for d in range(4)])


def gather_small(own, rows, columns):
    before = move(own, rows, columns)
    after = move(own, -rows, -columns)
    far = move(own, 2 * rows, 2 * columns)
    return jnp.stack([own, before, far, after])


def gather_large(own, rows, columns):
    before = move(own, rows, columns)
    after = move(own, -rows, -columns)
    far = move(before, rows, columns)
    return own, before, after, far


def reduce_large(own, before, after, far, rows, columns):
    full = jnp.float32
    after = move(after, rows, columns)
    far, own = lax.optimization_barrier((move(far, -rows, -columns), own))
    near = (before.astype(full) + far.astype(full)).astype(before.dtype)
    before = move(near, -rows, -columns)
    return own + before.astype(full) + after.astype(full)


def reduce_small(terms, rows, columns):
    full, low = jnp.float32, terms.astype(jnp.bfloat16)
    far = move(low[2], -2 * rows, -2 * columns)
    before = move(low[1], -rows, -columns)
    after = move(low[3], rows, columns)
    return terms[0] + far.astype(full) + before.astype(full) + after.astype(full)


SETS, WORDS, ROOM = 3, 6, 40
NONE = -2 * BLOCK


def plan(sel, place, qd_own, qd_far, table, qd, count, *, pairs):
    for half, part in enumerate((qd_own, qd_far)):
        for g in range(pairs // 2):
            for n in range(2):
                qd[n, half * (pairs // 2) + g] = part[n, g]
    row, column = place[0], place[1]

    def put(c, word, at, value):
        table[(c * WORDS + word) * ROOM + at] = jnp.int32(value)

    for c in range(SETS):
        count[c] = 0
    for pair in range(pairs):
        for s in range(sel.shape[1]):
            block = sel[pair, s]
            y, x = (block >> 2) & 3, block & 3
            if (pair >> 1) & 1 == 0:
                distance, other = (row - y) & 3, (column - x) & 3
            else:
                distance, other = (column - x) & 3, (row - y) & 3
            c = jnp.where(distance == 0, 2, jnp.where(distance == 2, 1, 0))
            at = count[c]
            word = (at & 1) * 2
            put(c, 0, at >> 1, pair)
            put(c, word + 1, at >> 1, other + jnp.where(distance == 3, SIDE, 0))
            put(c, word + 2, at >> 1, 0 if s == 0 else BLOCK)
            count[c] = at + (block >= 0).astype(jnp.int32)
        for c in range(SETS):
            at = count[c]
            put(c, 3, at >> 1, 0)
            put(c, 4, at >> 1, NONE)
            count[c] = at + (at & 1)
    for c in range(SETS):
        at = count[c] >> 1
        for word, value in enumerate((0, 0, NONE, 0, NONE)):
            put(c, word, at, value)
        put(c, 5, 0, at)


def plan_call(sel, place, qd_own, qd_far):
    vmem = pl.BlockSpec(memory_space=pltpu.VMEM)
    smem = pl.BlockSpec(memory_space=pltpu.SMEM)
    pairs = sel.shape[0]
    shape = (2, pairs) + qd_own.shape[2:]
    return pl.pallas_call(
        lambda *refs: plan(*refs, pairs=pairs),
        out_shape=[
            jax.ShapeDtypeStruct((SETS * WORDS * ROOM,), jnp.int32),
            jax.ShapeDtypeStruct(shape, qd_own.dtype),
        ],
        in_specs=[smem, smem, vmem, vmem],
        out_specs=[smem, vmem],
        scratch_shapes=[pltpu.SMEM((SETS + 1,), jnp.int32)],
        name="plan",
        compiler_params=pltpu.CompilerParams(vmem_limit_bytes=8 << 20),
        cost_estimate=pl.CostEstimate(flops=1 << 20, bytes_accessed=4 << 20, transcendentals=0),
    )(sel, place, qd_own, qd_far)


def attend(table, place, stats, qd, *refs, which, parts, scale, pairs, first, final):
    half_rows = BLOCK // 2
    half_pairs = pairs // 2
    low, full = jnp.bfloat16, jnp.float32
    given = refs[: 2 * parts]
    refs = refs[2 * parts :]
    if not first:
        dq_in, refs = refs[0], refs[1:]
    terms, refs = refs[: 2 * parts], refs[2 * parts :]
    if final:
        dq_own, dq_far, dq_t = refs[0], refs[1], refs[-1]
        rows, acc, p_even, s_even, p_odd, s_odd = refs[2:-1]
    else:
        dq_t = refs[0]
        rows, acc, p_even, s_even, p_odd, s_odd = refs[1:]
    blocks = parts * SIDE

    def word(n, at):
        return table[(which * WORDS + n) * ROOM + at]

    total = word(5, 0)
    if first:
        dq_t[...] = jnp.zeros_like(dq_t)
    else:
        dq_t[...] = dq_in[...]

    def slot(head, n, r):
        return (head * blocks + n * SIDE + r) * 2

    for head in range(2):
        for n in range(parts):
            for r in range(SIDE):
                for kv in range(2):
                    at = slot(head, n, r) + kv
                    rows[at] = given[head * parts + n][r, kv * half_rows : (kv + 1) * half_rows]
                    acc[at] = jnp.zeros(acc.shape[1:], full)

    at_row = lax.broadcasted_iota(jnp.int32, (half_rows, BLOCK), 0)
    at_query = lax.broadcasted_iota(jnp.int32, (half_rows, BLOCK), 1)
    quarter = BLOCK // 4
    offset = at_row + place[2] * quarter + jnp.where(at_row >= quarter, quarter, 0) - at_query

    def across(one, two, dim):
        return lax.dot_general(one, two, (((dim,), (dim,)), ((), ())), preferred_element_type=full)

    def item(n):
        pair = word(0, n)
        base = ((pair >> 1) & 1) * blocks
        return pair, (base + word(1, n)) * 2, (base + word(3, n)) * 2

    def weigh(n, p_buf, s_buf):
        pair, one, two = item(n)
        lse = stats[pl.ds(pair, 1), :]
        delta = stats[pl.ds(pair + pairs, 1), :]
        k = jnp.concatenate([rows[one], rows[two]], axis=0)
        scores = across(k, qd[0, pair], 1) * scale
        keep = jnp.concatenate([offset <= word(2, n), offset <= word(4, n)], axis=0)
        probs = jnp.where(keep, jnp.exp(scores - lse), 0.0)
        p_buf[...] = probs.astype(low)
        v = jnp.concatenate([rows[one + 1], rows[two + 1]], axis=0)
        dprobs = across(v, qd[1, pair], 1)
        s_buf[...] = (probs * (dprobs - delta) * scale).astype(low)

    def spread(n, p_buf, s_buf):
        pair, one, two = item(n)
        dv = jnp.dot(p_buf[...], qd[1, pair], preferred_element_type=full)
        acc[one + 1] += dv[:half_rows]
        acc[two + 1] += dv[half_rows:]
        dk = jnp.dot(s_buf[...], qd[0, pair], preferred_element_type=full)
        acc[one] += dk[:half_rows]
        acc[two] += dk[half_rows:]
        k = jnp.concatenate([rows[one], rows[two]], axis=0)
        dq_t[pair] += across(k, s_buf[...], 0)

    @pl.when(total > 0)
    def _():
        weigh(0, p_even, s_even)
        steps = (total + 1) >> 1

        @pl.loop(0, steps - 1)
        def _(i):
            weigh(2 * i + 1, p_odd, s_odd)
            spread(2 * i, p_even, s_even)
            weigh(2 * i + 2, p_even, s_even)
            spread(2 * i + 1, p_odd, s_odd)

        last = 2 * steps - 2
        weigh(last + 1, p_odd, s_odd)
        spread(last, p_even, s_even)
        spread(last + 1, p_odd, s_odd)

    for head in range(2):
        for n in range(parts):
            out = terms[head * parts + n]
            for r in range(SIDE):
                for kv in range(2):
                    out[r, kv * half_rows : (kv + 1) * half_rows] = acc[slot(head, n, r) + kv].astype(
                        out.dtype
                    )
    if final:
        for g in range(half_pairs):
            dq_own[g] = dq_t[g].T
            dq_far[g] = dq_t[half_pairs + g].T.astype(low)


def attend_call(which, table, place, stats, qd, given, dq, final):
    low, full = jnp.bfloat16, jnp.float32
    vmem = pl.BlockSpec(memory_space=pltpu.VMEM)
    smem = pl.BlockSpec(memory_space=pltpu.SMEM)
    parts = len(given) // 2
    pairs, head_dim = qd.shape[1], qd.shape[-1]
    first = dq is None
    share = 8 * parts
    term = jax.ShapeDtypeStruct(given[0].shape, full if final else low)
    dq_shape = jax.ShapeDtypeStruct((pairs, head_dim, BLOCK), full)
    if final:
        dq_outs = [
            jax.ShapeDtypeStruct((pairs // 2, BLOCK, head_dim), full),
            jax.ShapeDtypeStruct((pairs // 2, BLOCK, head_dim), low),
        ]
    else:
        dq_outs = [dq_shape]
    held = parts * SIDE * 4
    square = pltpu.VMEM((BLOCK, BLOCK), low)
    scratch = [
        pltpu.VMEM((held, BLOCK // 2, head_dim), low),
        pltpu.VMEM((held, BLOCK // 2, head_dim), full),
        square,
        square,
        square,
        square,
    ]
    if final:
        scratch.append(pltpu.VMEM((pairs, head_dim, BLOCK), full))
    operands = (table, place, stats, qd, *given) + (() if first else (dq,))
    outs = pl.pallas_call(
        lambda *refs: attend(
            *refs,
            which=which,
            parts=parts,
            scale=head_dim**-0.5,
            pairs=pairs,
            first=first,
            final=final,
        ),
        out_shape=[term] * len(given) + dq_outs,
        in_specs=[smem, smem] + [vmem] * (len(operands) - 2),
        out_specs=[vmem] * (len(given) + len(dq_outs)),
        scratch_shapes=scratch,
        compiler_params=pltpu.CompilerParams(vmem_limit_bytes=20 << 20),
        cost_estimate=pl.CostEstimate(
            flops=share * 5 * 2 * BLOCK * BLOCK * head_dim,
            bytes_accessed=(2 * parts + 4) << 20,
            transcendentals=share * BLOCK * BLOCK,
        ),
    )(*operands)
    return outs[: len(given)], outs[len(given) :]


def step(queries, key_rows, value_rows, forward_out, grad_out, logsumexp, selected):
    rows, heads, members, head_dim = queries.shape
    pairs = heads * members
    low, full = jnp.bfloat16, jnp.float32
    ctx, dp = lax.axis_index("ctx"), lax.axis_index("dp")
    lower = dp < 2

    kv = jnp.stack([key_rows, value_rows]).transpose(2, 0, 1, 3)
    far = swap(kv, 2)
    kv = jnp.where(lower, jnp.concatenate([kv, far], 2), jnp.concatenate([far, kv], 2))
    kv = kv.reshape(heads, BLOCK, head_dim)

    qd_own = jnp.stack([queries, grad_out]).transpose(0, 2, 3, 1, 4).reshape(2, pairs, rows, head_dim)
    qd_far = swap(qd_own, 1)

    own_0, before_0, after_0, far_0 = gather_large(gather_small(kv[0], 0, 1), 1, 0)
    own_1, before_1, after_1, far_1 = gather_large(gather_small(kv[1], 1, 0), 0, 1)

    delta = jnp.sum(grad_out.astype(full) * forward_out.astype(full), axis=-1)
    delta = delta.transpose(1, 2, 0)
    ids = jnp.pad(selected[0].astype(full), ((0, 0), (0, 0), (0, BLOCK - selected.shape[-1])))
    small = jnp.stack([logsumexp, delta, ids]).reshape(3, pairs, BLOCK)
    small_far = swap(small, 1)
    small = jnp.concatenate([small, small_far], axis=1)
    stats = small[0:2].reshape(4 * pairs, BLOCK)
    sel = small[2, :, : selected.shape[-1]].astype(jnp.int32)
    place = jnp.stack([ctx // SIDE, ctx % SIDE, dp % 2]).astype(jnp.int32)

    table, qd = plan_call(sel, place, qd_own, qd_far)
    shared = (table, place, stats, qd)
    near_parts = (before_0, after_0, before_1, after_1)
    (before_0, after_0, before_1, after_1), (dq,) = attend_call(0, *shared, near_parts, None, False)
    (far_0, far_1), (dq,) = attend_call(1, *shared, (far_0, far_1), dq, False)
    (own_0, own_1), (dq_own, dq_far) = attend_call(2, *shared, (own_0, own_1), dq, True)

    dq_near = swap(dq_far, 1)
    query_grad = (dq_own + dq_near.astype(full)).astype(low)
    query_grad = query_grad.reshape(heads, members, rows, head_dim).transpose(2, 0, 1, 3)

    grad_0 = reduce_small(reduce_large(own_0, before_0, after_0, far_0, 1, 0), 0, 1)
    grad_1 = reduce_small(reduce_large(own_1, before_1, after_1, far_1, 0, 1), 1, 0)

    grads = jnp.stack([grad_0, grad_1]).reshape(heads, 2, 2, BLOCK // 4, head_dim)
    keep = jnp.where(lower, grads[:, :, 0], grads[:, :, 1])
    send = jnp.where(lower, grads[:, :, 1], grads[:, :, 0]).astype(low)
    grads = (keep + swap(send, 2).astype(full)).transpose(1, 2, 0, 3)
    return (query_grad, grads[0], grads[1])


def solution(mesh):
    return jax.shard_map(
        step,
        mesh=mesh,
        in_specs=(
            P("ctx", "head", "dp", None),
            P(("ctx", "dp"), "head", None),
            P(("ctx", "dp"), "head", None),
            P("ctx", "head", "dp", None),
            P("ctx", "head", "dp", None),
            P("head", "dp", "ctx"),
            P("ctx", "head", "dp", None),
        ),
        out_specs=(
            P("ctx", "head", "dp", None),
            P(("ctx", "dp"), "head", None),
            P(("ctx", "dp"), "head", None),
        ),
        check_vma=False,
    )
```

```python
import jax
import jax.numpy as jnp
from jax import lax
from jax.experimental import pallas as pl
from jax.experimental.pallas import tpu as pltpu
from jax.sharding import PartitionSpec as P


BLOCK = 256
SIDE = 4


def shifts(rows, columns):
    return [
        (y * SIDE + x, (y + rows) % SIDE * SIDE + (x + columns) % SIDE)
        for y in range(SIDE)
        for x in range(SIDE)
    ]


def move(array, rows, columns):
    return lax.ppermute(array, "ctx", shifts(rows, columns))


def swap(array, bit):
    return lax.ppermute(array, "dp", [(d, d ^ bit) for d in range(4)])


def gather_small(own, rows, columns):
    before = move(own, rows, columns)
    after = move(own, -rows, -columns)
    far = move(own, 2 * rows, 2 * columns)
    return jnp.stack([own, before, far, after])


def gather_large(own, rows, columns):
    before = move(own, rows, columns)
    after = move(own, -rows, -columns)
    far = move(before, rows, columns)
    return own, before, after, far


def reduce_large(own, before, after, far, rows, columns):
    full = jnp.float32
    after = move(after, rows, columns)
    far, own = lax.optimization_barrier((move(far, -rows, -columns), own))
    near = (before.astype(full) + far.astype(full)).astype(before.dtype)
    before = move(near, -rows, -columns)
    return own + before.astype(full) + after.astype(full)


def reduce_small(terms, rows, columns):
    full, low = jnp.float32, terms.astype(jnp.bfloat16)
    far = move(low[2], -2 * rows, -2 * columns)
    before = move(low[1], -rows, -columns)
    after = move(low[3], rows, columns)
    return terms[0] + far.astype(full) + before.astype(full) + after.astype(full)


SETS, WORDS, ROOM = 3, 6, 40
NONE = -2 * BLOCK


def plan(sel, place, qd_own, qd_far, table, qd, count, *, pairs):
    for half, part in enumerate((qd_own, qd_far)):
        for g in range(pairs // 2):
            for n in range(2):
                qd[n, half * (pairs // 2) + g] = part[n, g]
    row, column = place[0], place[1]

    def put(c, word, at, value):
        table[(c * WORDS + word) * ROOM + at] = jnp.int32(value)

    for c in range(SETS):
        count[c] = 0
    for pair in range(pairs):
        for s in range(sel.shape[1]):
            block = sel[pair, s]
            y, x = (block >> 2) & 3, block & 3
            if (pair >> 1) & 1 == 0:
                distance, other = (row - y) & 3, (column - x) & 3
            else:
                distance, other = (column - x) & 3, (row - y) & 3
            c = jnp.where(distance == 0, 2, jnp.where(distance == 2, 1, 0))
            at = count[c]
            word = (at & 1) * 2
            put(c, 0, at >> 1, pair)
            put(c, word + 1, at >> 1, other + jnp.where(distance == 3, SIDE, 0))
            put(c, word + 2, at >> 1, 0 if s == 0 else BLOCK)
            count[c] = at + (block >= 0).astype(jnp.int32)
        for c in range(SETS):
            at = count[c]
            put(c, 3, at >> 1, 0)
            put(c, 4, at >> 1, NONE)
            count[c] = at + (at & 1)
    for c in range(SETS):
        at = count[c] >> 1
        for word, value in enumerate((0, 0, NONE, 0, NONE)):
            put(c, word, at, value)
        put(c, 5, 0, at)


def plan_call(sel, place, qd_own, qd_far):
    vmem = pl.BlockSpec(memory_space=pltpu.VMEM)
    smem = pl.BlockSpec(memory_space=pltpu.SMEM)
    pairs = sel.shape[0]
    shape = (2, pairs) + qd_own.shape[2:]
    return pl.pallas_call(
        lambda *refs: plan(*refs, pairs=pairs),
        out_shape=[
            jax.ShapeDtypeStruct((SETS * WORDS * ROOM,), jnp.int32),
            jax.ShapeDtypeStruct(shape, qd_own.dtype),
        ],
        in_specs=[smem, smem, vmem, vmem],
        out_specs=[smem, vmem],
        scratch_shapes=[pltpu.SMEM((SETS + 1,), jnp.int32)],
        name="plan",
        compiler_params=pltpu.CompilerParams(vmem_limit_bytes=8 << 20),
        cost_estimate=pl.CostEstimate(flops=1 << 20, bytes_accessed=4 << 20, transcendentals=0),
    )(sel, place, qd_own, qd_far)


def attend(table, place, stats, qd, *refs, which, parts, scale, pairs, first, final):
    half_rows = BLOCK // 2
    half_pairs = pairs // 2
    low, full = jnp.bfloat16, jnp.float32
    given = refs[: 2 * parts]
    refs = refs[2 * parts :]
    if not first:
        dq_in, refs = refs[0], refs[1:]
    terms, refs = refs[: 2 * parts], refs[2 * parts :]
    if final:
        dq_own, dq_far, dq_t = refs[0], refs[1], refs[-1]
        rows, acc, p_even, s_even, p_odd, s_odd = refs[2:-1]
    else:
        dq_t = refs[0]
        rows, acc, p_even, s_even, p_odd, s_odd = refs[1:]
    blocks = parts * SIDE

    def word(n, at):
        return table[(which * WORDS + n) * ROOM + at]

    total = word(5, 0)
    if first:
        dq_t[...] = jnp.zeros_like(dq_t)
    else:
        dq_t[...] = dq_in[...]

    def slot(head, n, r):
        return (head * blocks + n * SIDE + r) * 2

    for head in range(2):
        for n in range(parts):
            for r in range(SIDE):
                for kv in range(2):
                    at = slot(head, n, r) + kv
                    rows[at] = given[head * parts + n][r, kv * half_rows : (kv + 1) * half_rows]
                    acc[at] = jnp.zeros(acc.shape[1:], full)

    at_row = lax.broadcasted_iota(jnp.int32, (half_rows, BLOCK), 0)
    at_query = lax.broadcasted_iota(jnp.int32, (half_rows, BLOCK), 1)
    quarter = BLOCK // 4
    offset = at_row + place[2] * quarter + jnp.where(at_row >= quarter, quarter, 0) - at_query

    def across(one, two, dim):
        return lax.dot_general(one, two, (((dim,), (dim,)), ((), ())), preferred_element_type=full)

    def item(n):
        pair = word(0, n)
        base = ((pair >> 1) & 1) * blocks
        return pair, (base + word(1, n)) * 2, (base + word(3, n)) * 2

    def weigh(n, p_buf, s_buf):
        pair, one, two = item(n)
        lse = stats[pl.ds(pair, 1), :]
        delta = stats[pl.ds(pair + pairs, 1), :]
        k = jnp.concatenate([rows[one], rows[two]], axis=0)
        scores = across(k, qd[0, pair], 1) * scale
        keep = jnp.concatenate([offset <= word(2, n), offset <= word(4, n)], axis=0)
        probs = jnp.where(keep, jnp.exp(scores - lse), 0.0)
        p_buf[...] = probs.astype(low)
        v = jnp.concatenate([rows[one + 1], rows[two + 1]], axis=0)
        dprobs = across(v, qd[1, pair], 1)
        s_buf[...] = (probs * (dprobs - delta) * scale).astype(low)

    def spread(n, p_buf, s_buf):
        pair, one, two = item(n)
        dv = jnp.dot(p_buf[...], qd[1, pair], preferred_element_type=full)
        acc[one + 1] += dv[:half_rows]
        acc[two + 1] += dv[half_rows:]
        dk = jnp.dot(s_buf[...], qd[0, pair], preferred_element_type=full)
        acc[one] += dk[:half_rows]
        acc[two] += dk[half_rows:]
        k = jnp.concatenate([rows[one], rows[two]], axis=0)
        dq_t[pair] += across(k, s_buf[...], 0)

    @pl.when(total > 0)
    def _():
        weigh(0, p_even, s_even)
        steps = (total + 1) >> 1

        @pl.loop(0, steps - 1)
        def _(i):
            weigh(2 * i + 1, p_odd, s_odd)
            spread(2 * i, p_even, s_even)
            weigh(2 * i + 2, p_even, s_even)
            spread(2 * i + 1, p_odd, s_odd)

        last = 2 * steps - 2
        weigh(last + 1, p_odd, s_odd)
        spread(last, p_even, s_even)
        spread(last + 1, p_odd, s_odd)

    for head in range(2):
        for n in range(parts):
            out = terms[head * parts + n]
            for r in range(SIDE):
                for kv in range(2):
                    out[r, kv * half_rows : (kv + 1) * half_rows] = acc[slot(head, n, r) + kv].astype(
                        out.dtype
                    )
    if final:
        for g in range(half_pairs):
            dq_own[g] = dq_t[g].T
            dq_far[g] = dq_t[half_pairs + g].T.astype(low)


def attend_call(which, table, place, stats, qd, given, dq, final):
    low, full = jnp.bfloat16, jnp.float32
    vmem = pl.BlockSpec(memory_space=pltpu.VMEM)
    smem = pl.BlockSpec(memory_space=pltpu.SMEM)
    parts = len(given) // 2
    pairs, head_dim = qd.shape[1], qd.shape[-1]
    first = dq is None
    share = 8 * parts
    term = jax.ShapeDtypeStruct(given[0].shape, full if final else low)
    dq_shape = jax.ShapeDtypeStruct((pairs, head_dim, BLOCK), full)
    if final:
        dq_outs = [
            jax.ShapeDtypeStruct((pairs // 2, BLOCK, head_dim), full),
            jax.ShapeDtypeStruct((pairs // 2, BLOCK, head_dim), low),
        ]
    else:
        dq_outs = [dq_shape]
    held = parts * SIDE * 4
    square = pltpu.VMEM((BLOCK, BLOCK), low)
    scratch = [
        pltpu.VMEM((held, BLOCK // 2, head_dim), low),
        pltpu.VMEM((held, BLOCK // 2, head_dim), full),
        square,
        square,
        square,
        square,
    ]
    if final:
        scratch.append(pltpu.VMEM((pairs, head_dim, BLOCK), full))
    operands = (table, place, stats, qd, *given) + (() if first else (dq,))
    outs = pl.pallas_call(
        lambda *refs: attend(
            *refs,
            which=which,
            parts=parts,
            scale=head_dim**-0.5,
            pairs=pairs,
            first=first,
            final=final,
        ),
        out_shape=[term] * len(given) + dq_outs,
        in_specs=[smem, smem] + [vmem] * (len(operands) - 2),
        out_specs=[vmem] * (len(given) + len(dq_outs)),
        scratch_shapes=scratch,
        compiler_params=pltpu.CompilerParams(vmem_limit_bytes=20 << 20),
        cost_estimate=pl.CostEstimate(
            flops=share * 5 * 2 * BLOCK * BLOCK * head_dim,
            bytes_accessed=(2 * parts + 4) << 20,
            transcendentals=share * BLOCK * BLOCK,
        ),
    )(*operands)
    return outs[: len(given)], outs[len(given) :]


def step(queries, key_rows, value_rows, forward_out, grad_out, logsumexp, selected):
    rows, heads, members, head_dim = queries.shape
    pairs = heads * members
    low, full = jnp.bfloat16, jnp.float32
    ctx, dp = lax.axis_index("ctx"), lax.axis_index("dp")
    lower = dp < 2

    kv = jnp.stack([key_rows, value_rows]).transpose(2, 0, 1, 3)
    far = swap(kv, 2)
    kv = jnp.where(lower, jnp.concatenate([kv, far], 2), jnp.concatenate([far, kv], 2))
    kv = kv.reshape(heads, BLOCK, head_dim)

    qd_own = jnp.stack([queries, grad_out]).transpose(0, 2, 3, 1, 4).reshape(2, pairs, rows, head_dim)
    qd_far = swap(qd_own, 1)

    own_0, before_0, after_0, far_0 = gather_large(gather_small(kv[0], 0, 1), 1, 0)
    own_1, before_1, after_1, far_1 = gather_large(gather_small(kv[1], 1, 0), 0, 1)

    delta = jnp.sum(grad_out.astype(full) * forward_out.astype(full), axis=-1)
    delta = delta.transpose(1, 2, 0)
    ids = jnp.pad(selected[0].astype(full), ((0, 0), (0, 0), (0, BLOCK - selected.shape[-1])))
    small = jnp.stack([logsumexp, delta, ids]).reshape(3, pairs, BLOCK)
    small_far = swap(small, 1)
    small = jnp.concatenate([small, small_far], axis=1)
    stats = small[0:2].reshape(4 * pairs, BLOCK)
    sel = small[2, :, : selected.shape[-1]].astype(jnp.int32)
    place = jnp.stack([ctx // SIDE, ctx % SIDE, dp % 2]).astype(jnp.int32)

    table, qd = plan_call(sel, place, qd_own, qd_far)
    shared = (table, place, stats, qd)
    near_parts = (before_0, after_0, before_1, after_1)
    (before_0, after_0, before_1, after_1), (dq,) = attend_call(0, *shared, near_parts, None, False)
    (far_0, far_1), (dq,) = attend_call(1, *shared, (far_0, far_1), dq, False)
    (own_0, own_1), (dq_own, dq_far) = attend_call(2, *shared, (own_0, own_1), dq, True)

    dq_near = swap(dq_far, 1)
    query_grad = (dq_own + dq_near.astype(full)).astype(low)
    query_grad = query_grad.reshape(heads, members, rows, head_dim).transpose(2, 0, 1, 3)

    grad_0 = reduce_small(reduce_large(own_0, before_0, after_0, far_0, 1, 0), 0, 1)
    grad_1 = reduce_small(reduce_large(own_1, before_1, after_1, far_1, 0, 1), 1, 0)

    grads = jnp.stack([grad_0, grad_1]).reshape(heads, 2, 2, BLOCK // 4, head_dim)
    keep = jnp.where(lower, grads[:, :, 0], grads[:, :, 1])
    send = jnp.where(lower, grads[:, :, 1], grads[:, :, 0]).astype(low)
    far = swap(send, 2).astype(full)
    key_grad, value_grad = (
        jnp.stack([keep[a, n] + far[a, n] for a in range(heads)], axis=1) for n in range(2)
    )
    return (query_grad, key_grad, value_grad)


def solution(mesh):
    return jax.shard_map(
        step,
        mesh=mesh,
        in_specs=(
            P("ctx", "head", "dp", None),
            P(("ctx", "dp"), "head", None),
            P(("ctx", "dp"), "head", None),
            P("ctx", "head", "dp", None),
            P("ctx", "head", "dp", None),
            P("head", "dp", "ctx"),
            P("ctx", "head", "dp", None),
        ),
        out_specs=(
            P("ctx", "head", "dp", None),
            P(("ctx", "dp"), "head", None),
            P(("ctx", "dp"), "head", None),
        ),
        check_vma=False,
    )
```
